32 devices in a mesh: rep: 2 (over y), grp: 4 (over z), sub: 4 (over x, core).
Axes of the slice: x: 2, y: 2, z: 4, core: 2. Of those that a mesh axis runs over, the one named last changes fastest.
Arguments:
- embeddings: bfloat16 [8192, 1024], P(('rep', 'grp', 'sub')), parts along dimension 0, may hold values from -6 to 6
- cluster_ids: int32 [8192, 1], P(('rep', 'grp', 'sub')), parts along dimension 0, may hold values from 0 to 3; in each aligned block of 256 rows (0 to 255, 256 to 511, ...) at most 128 rows name the same one
Outputs:
- max_similarity: float32 [8192], P(('rep', 'grp', 'sub')), parts along dimension 0
The draws below stay inside these ranges and needn't reach their ends.
There are 2 independent parts, one for each index of `rep`. The reference program is written for one: setup_inputs(seed, part) draws one part's arguments, and reference() takes and returns one part's arrays. A program takes and returns all parts, laid end to end along the dimension named above; each array names one. Nothing has to cross between parts.
Inputs may be any that keep to these rules, and one draw needn't show every extreme that they name: `cluster_ids`: cluster numbers run from 0 to 3; among the rows of one device no cluster is named by more than 128 rows, and in every draw some cluster is named by exactly 128 rows of some device.
All inputs are finite; a program needn't handle non-finite values.
Results may differ from the reference program's by a relative error of at most 0.0014.
Values may be sent and summed in bfloat16 or wider, within the bound.
A program may use at most 64 MiB of HBM per device.

```python
import math
import jax
import jax.numpy as jnp
import numpy as np
from jax import lax

D = 1024
ROWS_DEV = 256
CAP = 128
CLUSTERS = 4
DOCS = 4096
N_GRP = 4
N_SUB = 4


def shard_levels(key, shape, pieces, smallest, top_value):
    loudness = 1.0
    for axis_at, blocks in pieces:
        heights = jax.random.uniform(jax.random.fold_in(jax.random.fold_in(key, 6), axis_at), (blocks,), jnp.float32, smallest / len(pieces), top_value / len(pieces))
        loudness = loudness * jnp.repeat(jnp.exp(heights), shape[axis_at] // blocks).reshape((-1,) + (1,) * (len(shape) - 1 - axis_at))
    return loudness


def shared_out(key, own, number, rows, number_of, top, reach, lean):
    sequence = jax.random.permutation(key, number_of)
    crowded, common = load_shares(number_of, rows * top, reach, lean, True), load_shares(number_of, rows * top, reach, lean, False)
    places = jnp.arange(number_of)

    def named(sizes, turn):
        used = int((sizes > 0).sum())
        fixed = max(1, used // 4)
        passed = fixed + (places - fixed + turn * (used - fixed)) % max(1, number_of - fixed)
        return jnp.zeros((number_of,), jnp.int32).at[sequence[jnp.where(places < fixed, places, passed)]].set(jnp.asarray(sizes, jnp.int32))

    sizes = jnp.where(number % 4 == 0, named(crowded, number // 4), named(common, number - number // 4 - 1))
    mixed = jax.random.permutation(jax.random.fold_in(own, 3), number_of)
    source_of, sink = mixed[0:number_of // 2 * 2:2], mixed[1:number_of // 2 * 2:2]
    slack = jnp.minimum(sizes[source_of] - 1, reach - sizes[sink]) // 2
    slack = jnp.where((source_of == sequence[0]) | (sink == sequence[0]) | (sizes[sink] == 0), 0, jnp.maximum(slack, 0))
    passed = jax.random.randint(jax.random.fold_in(own, 4), (number_of // 2,), 0, 1 << 20) % (slack + 1)
    sizes = sizes.at[source_of].add(-passed).at[sink].add(passed)
    items = jnp.searchsorted(jnp.cumsum(sizes), jnp.arange(rows * top), side="right").astype(jnp.int32)
    table = items.reshape(top, rows).T
    table = table[jax.random.permutation(jax.random.fold_in(own, 1), rows)]
    turn = jax.random.randint(jax.random.fold_in(own, 2), (rows, 1), 0, top)
    return jnp.take_along_axis(table, (jnp.arange(top)[None, :] + turn) % top, axis=1)


def load_shares(number_of, total, limit, skew, full):
    portions = [(1 << 20) // math.isqrt(grade ** skew) + 1 for grade in range(1, number_of + 1)]
    largest = limit if full else min(limit, max(-(-total // number_of), total * portions[0] // sum(portions)))
    least = 1 if total - largest >= number_of - 1 else 0
    given, surplus = [largest] + [least] * (number_of - 1), total - largest - least * (number_of - 1)
    while surplus > 0:
        candidates = [i for i in range(1, number_of) if given[i] < largest] or [i for i in range(1, number_of) if given[i] < limit]
        mass, remaining = sum([portions[i] for i in candidates]), surplus
        for i in candidates:
            more = min(limit - given[i], max(1, remaining * portions[i] // mass), surplus)
            given[i] = given[i] + more
            surplus = surplus - more
    return np.array(given)


def centred(own_key, dims, width, reach, split=(), kind=jnp.bfloat16):
    loudness = shard_levels(own_key, dims, split, -0.22, 0.18) if split else 1.0
    result = jax.random.normal(own_key, dims, jnp.float32) * width * loudness
    return jnp.minimum(jnp.maximum(result, -reach), reach).astype(kind)


def setup_inputs(seed: int = 0, part: int = 0) -> dict:
    key_list = jax.random.split(jax.random.key(seed), 3)
    part_splits = jax.random.split(jax.random.fold_in(key_list[2], part), 3)
    embeddings = centred(part_splits[0], (DOCS, D), 1.0, 6.0, ((0, 16),))
    cluster_ids_keys = jax.random.split(jax.random.fold_in(part_splits[1], 1), DOCS // ROWS_DEV)
    cluster_ids_turns = jax.random.permutation(jax.random.fold_in(part_splits[1], 3), DOCS // ROWS_DEV)
    cluster_ids = jax.vmap(lambda own, number: shared_out(jax.random.fold_in(part_splits[1], 2), own, number, ROWS_DEV, CLUSTERS, 1, CAP, 2))(cluster_ids_keys, cluster_ids_turns).reshape((DOCS, 1))
    return dict(embeddings=embeddings, cluster_ids=cluster_ids)


def reference(embeddings, cluster_ids):
    floats = embeddings.astype(jnp.float32)
    unit_rows = (floats * lax.rsqrt(lax.optimization_barrier(jnp.mean(floats * floats, axis=1, keepdims=True)) + 1e-06) / math.sqrt(D)).astype(jnp.bfloat16)
    labels = cluster_ids[:, 0].astype(jnp.int32)
    doc_total = labels.shape[0]
    ordering = jnp.argsort(labels, stable=True).astype(jnp.int32)
    sorted_labels = labels[ordering]
    tallies = jax.ops.segment_sum(jnp.ones_like(labels), labels, CLUSTERS).astype(jnp.int32)
    offsets = (jnp.cumsum(tallies) - tallies).astype(jnp.int32)
    within = (jnp.arange(doc_total, dtype=jnp.int32) - offsets[sorted_labels]).astype(jnp.int32)
    longest = CAP * N_GRP * N_SUB
    packed = jnp.zeros((CLUSTERS, longest, D), embeddings.dtype).at[sorted_labels, within].set(unit_rows[ordering])
    occupied = jnp.zeros((CLUSTERS, longest), jnp.int32).at[sorted_labels, within].set(1)
    diagonal_mask = jnp.eye(longest, dtype=bool)

    def cluster_maxima(pair):
        members, present = pair
        values = members.astype(jnp.float32)
        similar = jnp.dot(values, values.T, precision=lax.Precision.HIGHEST, preferred_element_type=jnp.float32)
        allowed = (present[None, :] > 0) & jnp.logical_not(diagonal_mask)
        return lax.optimization_barrier(jnp.max(jnp.where(allowed, similar, jnp.float32(-1.0)), axis=1))
    highest = lax.map(cluster_maxima, (packed, occupied))
    picked = highest[sorted_labels, within]
    return jnp.zeros((doc_total,), jnp.float32).at[ordering].set(picked)
```

```python
import functools
import math

import jax
import jax.numpy as jnp
from jax import lax
from jax.experimental import pallas as pl
from jax.experimental.pallas import tpu as pltpu
from jax.sharding import PartitionSpec as P

LANES = 128
SUBLANES = 8
VMEM_BUDGET = 24 << 20
MESH = pl.DeviceIdType.MESH


def from_behind(value, axis, by):
    peers = lax.axis_size(axis)
    return lax.ppermute(value, axis, [(i, (i + by) % peers) for i in range(peers)])


def masked_maxima(left_rows, right_rows, right_present, excluded):
    similar = jnp.dot(left_rows, right_rows.T, preferred_element_type=jnp.float32)
    allowed = (right_present[None, :] > 0) & jnp.logical_not(excluded)
    return jnp.where(allowed, similar, jnp.float32(-1.0))


def unit_of(rows, features):
    floats = rows.astype(jnp.float32)
    return (
        floats
        * lax.rsqrt(jnp.mean(floats * floats, axis=1, keepdims=True) + 1e-06)
        / math.sqrt(features)
    ).astype(jnp.bfloat16)


def by_owner(embeddings, cluster_ids):
    rows_dev, features = embeddings.shape
    groups = lax.axis_size("grp")
    subgroup = lax.axis_size("sub")
    capacity = 2 * rows_dev // groups
    unit_rows = unit_of(embeddings, features)
    labels = cluster_ids[:, 0]
    member_table = (labels[:, None] == jnp.arange(groups, dtype=jnp.int32)[None, :]).astype(
        jnp.int32
    )
    running = jnp.cumsum(member_table, axis=0)
    within = jnp.sum(jnp.where(member_table > 0, running - 1, 0), axis=1)
    slot_index = labels * capacity + within
    outgoing = jnp.zeros((groups * capacity, features), jnp.bfloat16).at[slot_index].set(unit_rows)
    occupied = jnp.zeros((groups * capacity,), jnp.int32).at[slot_index].set(1)
    arrived, arrived_present = (
        lax.all_to_all(
            outgoing.reshape(groups, capacity, features),
            "grp",
            split_axis=0,
            concat_axis=0,
            tiled=True,
        ),
        lax.all_to_all(
            occupied.reshape(groups, capacity), "grp", split_axis=0, concat_axis=0, tiled=True
        ),
    )
    owned_rows = arrived.reshape(groups * capacity, features)
    present = arrived_present.reshape(groups * capacity)
    held = owned_rows.shape[0]
    positions = jnp.arange(held, dtype=jnp.int32)
    excluded = positions[:, None] == positions[None, :]
    highest = jnp.max(masked_maxima(owned_rows, owned_rows, present, excluded), axis=1)
    no_exclusion = jnp.zeros((held, held), dtype=bool)
    for offset in range(1, subgroup // 2 + 1):
        peer_rows, peer_present = from_behind((owned_rows, present), "sub", offset)
        scores = masked_maxima(owned_rows, peer_rows, peer_present, no_exclusion)
        highest = jnp.maximum(highest, jnp.max(scores, axis=1))
        if 2 * offset != subgroup:
            column_best = jnp.max(
                jnp.where(present[:, None] > 0, scores, jnp.float32(-1.0)), axis=0
            )
            returned_best = from_behind(column_best, "sub", -offset)
            highest = jnp.maximum(highest, returned_best)
    returned = lax.all_to_all(
        highest.reshape(groups, capacity), "grp", split_axis=0, concat_axis=0, tiled=True
    )
    return returned.reshape(groups * capacity)[slot_index]


def meet_kernel(
    groups, subgroup, chunks, pieces,
    emb_ref, ids_ref, out_ref,
    emb_in, level, foreign, relay, lane_ids, level_ids, ids_col, row_part, col_part,
    ret_out, ret_in, col_out, col_in,
    in_sem, ids_in, ids_send, ids_recv, lid_send, lid_recv,
    lvl_send, lvl_recv, fwd_send, own_send, z_send, z_recv,
    relay_send, relay_back, relay_recv, ret_send, ret_recv, col_send, col_recv,
):
    rows, features = emb_ref.shape
    size = rows // chunks
    load = rows // pieces
    share = chunks // 4
    pivot = groups // 2
    last = groups - 1
    rep = lax.axis_index("rep")
    depth = lax.axis_index("grp")
    z = depth * (1 - rep) + (last - depth) * rep
    s = lax.axis_index("sub")
    partner = s + 1 - 2 * lax.rem(s, 2)
    others = subgroup // 2
    across_y = {"rep": 1 - rep}

    def peer(k):
        return lax.rem(s + k, subgroup)

    def at(where):
        return {"grp": where * (1 - rep) + (last - where) * rep}

    def remote(src, dst, send, recv, where):
        return pltpu.make_async_remote_copy(
            src_ref=src, dst_ref=dst, send_sem=send, recv_sem=recv,
            device_id=where, device_id_type=MESH,
        )

    def slot(b):
        return pl.ds(pl.multiple_of(b * rows, rows), rows)

    def piece(b, p):
        return pl.ds(pl.multiple_of(b * rows + p * load, load), load)

    def own_chunk(k):
        return level.at[pl.ds(pl.multiple_of(s * rows + k * size, size), size), :]

    def part(k):
        return pl.ds(pl.multiple_of(k * size, size), size)

    def load_piece(p):
        where = pl.ds(pl.multiple_of(p * load, load), load)
        return pltpu.make_async_copy(emb_ref.at[where, :], emb_in.at[where, :], in_sem.at[p])

    for p in range(pieces):
        load_piece(p).start()
    ids_copy = pltpu.make_async_copy(ids_ref, level_ids.at[s], ids_in)
    ids_copy.start()

    barrier = pltpu.get_barrier_semaphore()
    for k in range(1, subgroup):
        pl.semaphore_signal(barrier, 1, device_id={"sub": peer(k)}, device_id_type=MESH)
    pl.semaphore_signal(barrier, 1, device_id=across_y, device_id_type=MESH)

    @pl.when(z > 0)
    def _():
        pl.semaphore_signal(barrier, 1, device_id=at(z - 1), device_id_type=MESH)

    @pl.when(z < last)
    def _():
        pl.semaphore_signal(barrier, 1, device_id=at(z + 1), device_id_type=MESH)

    col_part[...] = jnp.full(col_part.shape, -1.0, jnp.float32)

    def level_ids_copy(k, owner):
        return remote(ids_ref, level_ids.at[owner], lid_send.at[k], lid_recv.at[owner], {"sub": peer(k)})

    def own_ids(where):
        return remote(ids_ref, lane_ids.at[z], ids_send.at[z], ids_recv.at[z], at(where))

    def ids_on(i, where):
        return remote(lane_ids.at[i], lane_ids.at[i], ids_send.at[i], ids_recv.at[i], at(where))

    def own_along(k, where):
        return remote(own_chunk(k), foreign.at[z, part(k), :], own_send.at[k], z_recv.at[z, k], at(where))

    def own_across(k):
        return remote(own_chunk(k), relay.at[z, part(k), :], own_send.at[k], relay_recv.at[z, k], across_y)

    def passed_on(i, k, where):
        block = foreign.at[i, part(k), :]
        return remote(block, block, z_send.at[i, k], z_recv.at[i, k], at(where))

    def passed_across(i, k):
        return remote(
            foreign.at[i, part(k), :], relay.at[i, part(k), :], z_send.at[i, k], relay_recv.at[i, k],
            across_y,
        )

    def relayed(i, k):
        block = relay.at[i, part(k), :]
        return remote(block, block, relay_send.at[i, k], relay_recv.at[i, k], at(z - 1))

    def back_across(i, k):
        return remote(
            relay.at[i, part(k), :], foreign.at[i, part(k), :], relay_back.at[i, k], z_recv.at[i, k],
            across_y,
        )

    def level_piece(owner, p, send, where):
        block = level.at[piece(owner, p), :]
        return remote(block, block, send, lvl_recv.at[owner, p], {"sub": where})

    sends_right = z < pivot
    sends_left = z == last

    def start_own(k):
        @pl.when((z == 0) | (z == 1) & (k < 2 * share))
        def _():
            own_along(k, z + 1).start()

        @pl.when((z == 1) & (k >= 2 * share))
        def _():
            own_across(k).start()

        @pl.when(sends_left)
        def _():
            own_along(k, z - 1).start()

    step = 2 * size
    per_piece = load // step

    def normalize(h):
        where = pl.ds(pl.multiple_of(h * step, step), step)
        into = pl.ds(pl.multiple_of(s * rows + h * step, step), step)
        level[into, :] = unit_of(emb_in[where, :], features)

    def send_own(p):
        @pl.when(z != pivot)
        def _():
            lax.fori_loop(
                2 * per_piece * p, 2 * per_piece * (p + 1), lambda k, c: (start_own(k), c)[1], 0
            )

        for k in range(1, others):
            level_piece(s, p, lvl_send.at[k, p], peer(2 * k)).start()
        level_piece(s, p, lvl_send.at[0, p], partner).start()

    load_piece(0).wait()
    lax.fori_loop(0, per_piece, lambda h, c: (normalize(h), c)[1], 0)
    neighbours = subgroup + (z > 0).astype(jnp.int32) + (z < last).astype(jnp.int32)
    pl.semaphore_wait(barrier, neighbours)
    for k in range(1, subgroup):
        level_ids_copy(k, s).start()

    @pl.when(sends_right)
    def _():
        own_ids(z + 1).start()

    @pl.when(sends_left)
    def _():
        own_ids(z - 1).start()

    send_own(0)

    def norm_step(p, carry):
        load_piece(p).wait()
        lax.fori_loop(p * per_piece, (p + 1) * per_piece, lambda h, c: (normalize(h), c)[1], 0)
        send_own(p)
        return carry

    lax.fori_loop(1, pieces, norm_step, 0)
    ids_copy.wait()

    def level_forward(p):
        for k in range(1, others):
            came_from = peer(2 * k)
            level_piece(came_from, p, lvl_send.at[0, p], s).wait_recv()
            level_piece(came_from, p, fwd_send.at[k, p], partner).start()

    def relay_step(j):
        block = 1 - j // (2 * share)
        chunk = lax.rem(j + 2 * share, chunks)
        hold = relayed(block, chunk)
        hold.wait_recv()

        @pl.when(z > 0)
        def _():
            hold.start()

        @pl.when((z == 0) | (z == 1) & (j >= share))
        def _():
            back_across(block, chunk).start()

    crossing = 3 * share

    def ticks(count, native, lag_relay, lag_level, relays=True):
        def tick(t, carry):
            native(t)
            if relays:
                j = t - lag_relay

                @pl.when((j >= 0) & (j < crossing))
                def _():
                    relay_step(j)

            p = t - lag_level

            @pl.when((p >= 0) & (lax.rem(p, share) == 0) & (p < pieces * share))
            def _():
                level_forward(p // share)

            return carry

        lax.fori_loop(0, count, tick, 0)

    def wait_chunks(i, low, high):
        lax.fori_loop(low, high, lambda k, c: (passed_on(i, k, z).wait_recv(), c)[1], 0)

    @pl.when(z == 0)
    def _():
        ticks(share * 3 + 3 * share, lambda t: None, 0, 3 * rep)

    @pl.when(z == 1)
    def _():
        ids_on(0, z).wait_recv()
        ids_on(0, z + 1).start()

        def native(k):
            @pl.when(k < chunks)
            def _():
                passed_on(0, k, z).wait_recv()

                @pl.when(k < share)
                def _():
                    passed_across(0, k).start()

                @pl.when(k >= share)
                def _():
                    passed_on(0, k, z + 1).start()

        ticks(chunks + share, native, 4 * (1 - rep), 4 - 2 * rep)

    @pl.when(z == pivot)
    def _():
        ids_on(1, z).wait_recv()
        ids_on(1, z + 1).start()

        def native(k):
            @pl.when(k < 2 * share)
            def _():
                passed_on(1, k, z).wait_recv()
                passed_on(1, k, z + 1).start()

            @pl.when((k >= 2 * share) & (k < 5 * share))
            def _():
                passed_on(0, k - share, z).wait_recv()
                passed_on(0, k - share, z + 1).start()

        ticks(5 * share, native, 0, 4)
        ids_on(0, z).wait_recv()
        ids_on(0, z + 1).start()
        ids_on(last, z).wait_recv()

    @pl.when(z == last)
    def _():
        def native(t):
            k = t + share

            @pl.when((t >= share) & (t < 2 * share))
            def _():
                passed_on(1, k, z).wait_recv()
                passed_on(1, k, z - 1).start()

        ticks(4 * share, native, 0, 0, relays=False)
        ids_on(0, z).wait_recv()
        ids_on(1, z).wait_recv()

    for p in range(pieces):
        for k in range(0, others):
            level_piece(lax.rem(partner + 2 * k, subgroup), p, lvl_send.at[0, p], s).wait_recv()
    for k in range(1, subgroup):
        level_ids_copy(k, peer(k)).wait_recv()

    def spread(i, ids):
        ids_col[i] = jnp.broadcast_to(ids, (LANES, rows)).T

    spread(z, level_ids[s])
    width = subgroup * rows

    def meet(i, low, high, own):
        count = high - low
        block = level[slot(s), :] if own else foreign[i, low:high, :]
        similar = lax.dot_general(
            block, level[...], (((1,), (1,)), ((), ())), preferred_element_type=jnp.float32
        )
        own_ids = ids_col[i, low:high, :]
        best = jnp.full((count, LANES), -1.0, jnp.float32)
        for col in range(0, width, LANES):
            same = own_ids == level_ids[col // rows, :, col % rows : col % rows + LANES]
            if own:
                across = lax.broadcasted_iota(jnp.int32, (rows, LANES), 1) + col
                down = lax.broadcasted_iota(jnp.int32, (rows, LANES), 0) + s * rows
                same = same & (across != down)
            kept = jnp.where(same, similar[:, col : col + LANES], jnp.float32(-1.0))
            best = jnp.maximum(best, kept)
            if not own:
                columns = jnp.max(kept.reshape(count // SUBLANES, SUBLANES, LANES), axis=0)
                col_part[:, col : col + LANES] = jnp.maximum(col_part[:, col : col + LANES], columns)
        row_part[i, low:high, :] = best

    def flat(i):
        return jnp.max(row_part[i].T, axis=0, keepdims=True)

    def ret_copy(i, owner, where):
        return remote(ret_out.at[i], ret_in.at[owner], ret_send.at[i], ret_recv.at[owner], at(where))

    def col_copy(k, owner):
        return remote(col_out.at[peer(k)], col_in.at[owner], col_send.at[k], col_recv.at[owner], {"sub": peer(k)})

    def give(i):
        ret_out[i] = flat(i)
        ret_copy(i, z, i).start()

    meet(z, 0, rows, True)

    half = rows // 2

    @pl.when(z == 1)
    def _():
        spread(0, lane_ids[0])
        meet(0, 0, rows, False)
        give(0)

    @pl.when(z == pivot)
    def _():
        spread(last, lane_ids[last])
        wait_chunks(last, 0, chunks)
        meet(last, 0, rows, False)
        give(last)
        spread(0, lane_ids[0])
        wait_chunks(0, 0, share)
        meet(0, 0, rows, False)
        give(0)
        spread(1, lane_ids[1])
        wait_chunks(1, 2 * share, chunks)
        meet(1, 0, rows, False)
        give(1)

    @pl.when(z == last)
    def _():
        spread(1, lane_ids[1])
        wait_chunks(1, 0, 2 * share)
        wait_chunks(1, 3 * share, chunks)
        meet(1, 0, rows, False)
        give(1)
        spread(0, lane_ids[0])
        wait_chunks(0, 0, 2 * share)
        meet(0, 0, half, False)
        wait_chunks(0, 2 * share, chunks)
        meet(0, half, rows, False)
        give(0)

    @pl.when(z > 0)
    def _():
        for b in range(subgroup):
            col_out[b] = jnp.max(col_part[:, b * rows : (b + 1) * rows], axis=0, keepdims=True)
        for k in range(1, subgroup):
            col_copy(k, s).start()

    best = flat(z)
    out_ref[...] = best.reshape(rows)

    for k in range(1, subgroup):
        level_ids_copy(k, s).wait_send()

    def sent_piece(p, carry):
        for k in range(1, others):
            level_piece(s, p, lvl_send.at[k, p], peer(2 * k)).wait_send()
            level_piece(peer(2 * k), p, fwd_send.at[k, p], partner).wait_send()
        level_piece(s, p, lvl_send.at[0, p], partner).wait_send()
        return carry

    lax.fori_loop(0, pieces, sent_piece, 0)

    def sent_chunks(copy, low, high):
        lax.fori_loop(low, high, lambda k, c: (copy(k).wait_send(), c)[1], 0)

    @pl.when(z != pivot)
    def _():
        own_ids(z).wait_send()
        sent_chunks(lambda k: own_along(k, z), 0, chunks)

    @pl.when(z == 1)
    def _():
        ids_on(0, z).wait_send()
        sent_chunks(lambda k: passed_on(0, k, z), 0, chunks)

    @pl.when(z == pivot)
    def _():
        ids_on(0, z).wait_send()
        ids_on(1, z).wait_send()
        sent_chunks(lambda k: passed_on(1, k, z), 0, 2 * share)
        sent_chunks(lambda k: passed_on(0, k, z), share, chunks)

    @pl.when(z == last)
    def _():
        sent_chunks(lambda k: passed_on(1, k, z), 2 * share, 3 * share)

    @pl.when((z > 0) & (z < last))
    def _():
        sent_chunks(lambda k: relayed(1, k), 2 * share, chunks)
        sent_chunks(lambda k: relayed(0, k), 0, share)

    @pl.when(z == 0)
    def _():
        sent_chunks(lambda k: back_across(1, k), 2 * share, 3 * share)

    @pl.when(z < pivot)
    def _():
        sent_chunks(lambda k: back_across(1, k), 3 * share, chunks)
        sent_chunks(lambda k: back_across(0, k), 0, share)

    @pl.when(z > 0)
    def _():
        out_ref[...] = jnp.maximum(out_ref[...], col_out[s].reshape(rows))
        for k in range(1, subgroup):
            col_copy(k, peer(k)).wait_recv()
            out_ref[...] = jnp.maximum(out_ref[...], col_in[peer(k)].reshape(rows))

    for j in range(1, groups):
        @pl.when((z < j) & (z < pivot) | (z > j) & (z > pivot) & (j >= pivot))
        def _(j=j):
            ret_copy(0, j, z).wait_recv()
            out_ref[...] = jnp.maximum(out_ref[...], ret_in[j].reshape(rows))

    @pl.when(z > 0)
    def _():
        for k in range(1, subgroup):
            col_copy(k, s).wait_send()
        ret_copy(0, z, 0).wait_send()

    @pl.when(z >= pivot)
    def _():
        ret_copy(1, z, 1).wait_send()

    @pl.when(z == pivot)
    def _():
        ret_copy(last, z, last).wait_send()


def by_meeting(embeddings, cluster_ids, chunks, pieces):
    rows, features = embeddings.shape
    groups = lax.axis_size("grp")
    subgroup = lax.axis_size("sub")
    dma = pltpu.SemaphoreType.DMA
    return pl.pallas_call(
        functools.partial(meet_kernel, groups, subgroup, chunks, pieces),
        out_shape=pltpu.VMEM((rows,), jnp.float32),
        in_specs=[pl.BlockSpec(memory_space=pl.ANY)] * 2,
        out_specs=pl.BlockSpec(memory_space=pltpu.VMEM),
        scratch_shapes=[
            pltpu.VMEM((rows, features), jnp.bfloat16),
            pltpu.VMEM((subgroup * rows, features), jnp.bfloat16),
            pltpu.VMEM((groups, rows, features), jnp.bfloat16),
            pltpu.VMEM((groups // 2, rows, features), jnp.bfloat16),
            pltpu.VMEM((groups, 1, rows), jnp.int32),
            pltpu.VMEM((subgroup, 1, rows), jnp.int32),
            pltpu.VMEM((groups, rows, LANES), jnp.int32),
            pltpu.VMEM((groups, rows, LANES), jnp.float32),
            pltpu.VMEM((SUBLANES, subgroup * rows), jnp.float32),
            pltpu.VMEM((groups, 1, rows), jnp.float32),
            pltpu.VMEM((groups, 1, rows), jnp.float32),
            pltpu.VMEM((subgroup, 1, rows), jnp.float32),
            pltpu.VMEM((subgroup, 1, rows), jnp.float32),
            dma((pieces,)), dma, dma((groups,)), dma((groups,)),
            dma((subgroup,)), dma((subgroup,)),
            dma((subgroup, pieces)), dma((subgroup, pieces)), dma((subgroup, pieces)),
            dma((chunks,)), dma((groups, chunks)), dma((groups, chunks)),
            dma((groups // 2, chunks)), dma((groups // 2, chunks)), dma((groups // 2, chunks)),
            dma((groups,)), dma((groups,)),
            dma((subgroup,)), dma((subgroup,)),
        ],
        compiler_params=pltpu.CompilerParams(collective_id=0, has_side_effects=True),
    )(embeddings, cluster_ids.reshape(1, rows))


def local(embeddings, cluster_ids):
    rows, features = embeddings.shape
    groups = lax.axis_size("grp")
    subgroup = lax.axis_size("sub")
    held = (groups + subgroup) * rows * features * embeddings.dtype.itemsize
    paired = lax.axis_size("rep") == 2 and subgroup % 2 == 0 and groups == 4
    if held <= VMEM_BUDGET and paired and rows % (LANES * 2) == 0:
        return by_meeting(embeddings, cluster_ids, rows // 16, 4)
    return by_owner(embeddings, cluster_ids)


def solution(mesh):
    return jax.shard_map(
        local,
        mesh=mesh,
        in_specs=(P(("rep", "grp", "sub"), None), P(("rep", "grp", "sub"), None)),
        out_specs=P(("rep", "grp", "sub")),
        check_vma=False,
    )
```

```python
import functools
import math

import jax
import jax.numpy as jnp
from jax import lax
from jax.experimental import pallas as pl
from jax.experimental.pallas import tpu as pltpu
from jax.sharding import PartitionSpec as P

LANES = 128
SUBLANES = 8
VMEM_BUDGET = 24 << 20
MESH = pl.DeviceIdType.MESH


def from_behind(value, axis, by):
    peers = lax.axis_size(axis)
    return lax.ppermute(value, axis, [(i, (i + by) % peers) for i in range(peers)])


def masked_maxima(left_rows, right_rows, right_present, excluded):
    similar = jnp.dot(left_rows, right_rows.T, preferred_element_type=jnp.float32)
    allowed = (right_present[None, :] > 0) & jnp.logical_not(excluded)
    return jnp.where(allowed, similar, jnp.float32(-1.0))


def unit_of(rows, features):
    floats = rows.astype(jnp.float32)
    return (
        floats
        * lax.rsqrt(jnp.mean(floats * floats, axis=1, keepdims=True) + 1e-06)
        / math.sqrt(features)
    ).astype(jnp.bfloat16)


def by_owner(embeddings, cluster_ids):
    rows_dev, features = embeddings.shape
    groups = lax.axis_size("grp")
    subgroup = lax.axis_size("sub")
    capacity = 2 * rows_dev // groups
    unit_rows = unit_of(embeddings, features)
    labels = cluster_ids[:, 0]
    member_table = (labels[:, None] == jnp.arange(groups, dtype=jnp.int32)[None, :]).astype(
        jnp.int32
    )
    running = jnp.cumsum(member_table, axis=0)
    within = jnp.sum(jnp.where(member_table > 0, running - 1, 0), axis=1)
    slot_index = labels * capacity + within
    outgoing = jnp.zeros((groups * capacity, features), jnp.bfloat16).at[slot_index].set(unit_rows)
    occupied = jnp.zeros((groups * capacity,), jnp.int32).at[slot_index].set(1)
    arrived, arrived_present = (
        lax.all_to_all(
            outgoing.reshape(groups, capacity, features),
            "grp",
            split_axis=0,
            concat_axis=0,
            tiled=True,
        ),
        lax.all_to_all(
            occupied.reshape(groups, capacity), "grp", split_axis=0, concat_axis=0, tiled=True
        ),
    )
    owned_rows = arrived.reshape(groups * capacity, features)
    present = arrived_present.reshape(groups * capacity)
    held = owned_rows.shape[0]
    positions = jnp.arange(held, dtype=jnp.int32)
    excluded = positions[:, None] == positions[None, :]
    highest = jnp.max(masked_maxima(owned_rows, owned_rows, present, excluded), axis=1)
    no_exclusion = jnp.zeros((held, held), dtype=bool)
    for offset in range(1, subgroup // 2 + 1):
        peer_rows, peer_present = from_behind((owned_rows, present), "sub", offset)
        scores = masked_maxima(owned_rows, peer_rows, peer_present, no_exclusion)
        highest = jnp.maximum(highest, jnp.max(scores, axis=1))
        if 2 * offset != subgroup:
            column_best = jnp.max(
                jnp.where(present[:, None] > 0, scores, jnp.float32(-1.0)), axis=0
            )
            returned_best = from_behind(column_best, "sub", -offset)
            highest = jnp.maximum(highest, returned_best)
    returned = lax.all_to_all(
        highest.reshape(groups, capacity), "grp", split_axis=0, concat_axis=0, tiled=True
    )
    return returned.reshape(groups * capacity)[slot_index]


LAG1 = (7, 4, 4, 4)
LAG2 = (2, 0, 4, 5, 2)


def meet_kernel(
    groups, subgroup, chunks, pieces,
    emb_ref, ids_ref, out_ref,
    emb_in, level, foreign, relay, lane_ids, level_ids, ids_col, row_part, col_part,
    ret_out, ret_in, col_out, col_in,
    in_sem, ids_in, ids_send, ids_recv, lid_recv,
    lvl_send, lvl_recv, mate_recv, own_send, pass_send, relay_send,
    first_recv, second_recv, bulk_recv, relay_recv, ret_send, ret_recv, col_recv,
):
    rows, features = emb_ref.shape
    size = rows // chunks
    load = rows // pieces
    far0 = chunks // 4
    far1 = 7 * chunks // 16
    near1 = chunks - far1
    pivot = groups // 2
    last = groups - 1
    rep = lax.axis_index("rep")
    depth = lax.axis_index("grp")
    z = depth * (1 - rep) + (last - depth) * rep
    s = lax.axis_index("sub")
    partner = s + 1 - 2 * lax.rem(s, 2)
    others = subgroup // 2
    across_y = {"rep": 1 - rep}

    def peer(k):
        return lax.rem(s + k, subgroup)

    def at(where):
        return {"grp": where * (1 - rep) + (last - where) * rep}

    def remote(src, dst, send, recv, where):
        return pltpu.make_async_remote_copy(
            src_ref=src, dst_ref=dst, send_sem=send, recv_sem=recv,
            device_id=where, device_id_type=MESH,
        )

    def slot(b):
        return pl.ds(pl.multiple_of(b * rows, rows), rows)

    def piece(b, p):
        return pl.ds(pl.multiple_of(b * rows + p * load, load), load)

    def own_chunk(k):
        return level.at[pl.ds(pl.multiple_of(s * rows + k * size, size), size), :]

    def part(k):
        return pl.ds(pl.multiple_of(k * size, size), size)

    def load_piece(p):
        where = pl.ds(pl.multiple_of(p * load, load), load)
        return pltpu.make_async_copy(emb_ref.at[where, :], emb_in.at[where, :], in_sem.at[p])

    for p in range(pieces):
        load_piece(p).start()
    ids_copy = pltpu.make_async_copy(ids_ref, level_ids.at[s], ids_in)
    ids_copy.start()

    barrier = pltpu.get_barrier_semaphore()
    for k in range(1, subgroup):
        pl.semaphore_signal(barrier, 1, device_id={"sub": peer(k)}, device_id_type=MESH)
    pl.semaphore_signal(barrier, 1, device_id=across_y, device_id_type=MESH)

    @pl.when(z > 0)
    def _():
        pl.semaphore_signal(barrier, 1, device_id=at(z - 1), device_id_type=MESH)

    @pl.when(z < last)
    def _():
        pl.semaphore_signal(barrier, 1, device_id=at(z + 1), device_id_type=MESH)

    @pl.when(z == last)
    def _():
        pl.semaphore_signal(barrier, 1, device_id=at(z - 1) | across_y, device_id_type=MESH)

    col_part[...] = jnp.full(col_part.shape, -1.0, jnp.float32)
    row_part[...] = jnp.full(row_part.shape, -1.0, jnp.float32)

    def level_ids_copy(k):
        return remote(ids_ref, level_ids.at[s], ids_send, lid_recv, {"sub": peer(k)})

    def own_ids(where):
        return remote(ids_ref, lane_ids.at[z], ids_send, ids_recv.at[z], at(where))

    def ids_on(i, where):
        return remote(lane_ids.at[i], lane_ids.at[i], ids_send, ids_recv.at[i], at(where))

    def bytes_of(count, send, recv):
        block = level.at[pl.ds(0, count), :]
        return remote(block, block, send, recv, {"sub": peer(1)})

    back0, back1, far1_recv, far0a, far0b, block3 = range(6)

    def own_along(k, where, recv):
        return remote(own_chunk(k), foreign.at[z, part(k), :], own_send, recv, at(where))

    def own_across(k):
        return remote(own_chunk(k), relay.at[1, part(k), :], own_send, relay_recv.at[k - near1], across_y)

    def passed_on(i, k, where, recv):
        block = foreign.at[i, part(k), :]
        return remote(block, block, pass_send, recv, at(where))

    def passed_across(k):
        return remote(
            foreign.at[0, part(k), :], relay.at[0, part(k), :], pass_send, relay_recv.at[far1 + k], across_y,
        )

    def relayed(i, k, j):
        block = relay.at[i, part(k), :]
        return remote(block, block, relay_send, relay_recv.at[j], at(z - 1))

    def returned(i, k, where):
        return remote(
            relay.at[i, part(k), :], foreign.at[i, part(k), :], relay_send, bulk_recv.at[back0 + i], where
        )

    def level_piece(owner, p, recv, where):
        block = level.at[piece(owner, p), :]
        return remote(block, block, lvl_send, recv, {"sub": where})

    sends_right = z < pivot
    sends_left = z == last

    def start_own(k):
        @pl.when(z == 0)
        def _():
            own_along(k, z + 1, first_recv.at[k]).start()

        @pl.when((z == 1) & (k < near1))
        def _():
            own_along(k, z + 1, second_recv.at[k]).start()

        @pl.when((z == 1) & (k >= near1))
        def _():
            own_across(k).start()

        @pl.when(sends_left)
        def _():
            own_along(k, z - 1, bulk_recv.at[block3]).start()

    step = 2 * size
    per_piece = load // step

    def normalize(h):
        where = pl.ds(pl.multiple_of(h * step, step), step)
        into = pl.ds(pl.multiple_of(s * rows + h * step, step), step)
        level[into, :] = unit_of(emb_in[where, :], features)

    def send_own(p):
        @pl.when(z != pivot)
        def _():
            lax.fori_loop(
                2 * per_piece * p, 2 * per_piece * (p + 1), lambda k, c: (start_own(k), c)[1], 0
            )

        for k in range(1, others):
            level_piece(s, p, lvl_recv.at[k, p], peer(2 * k)).start()
        level_piece(s, p, mate_recv.at[0], partner).start()

    load_piece(0).wait()
    lax.fori_loop(0, per_piece, lambda h, c: (normalize(h), c)[1], 0)
    neighbours = subgroup + sum(c.astype(jnp.int32) for c in (z > 0, z < last, z == 1))
    pl.semaphore_wait(barrier, neighbours)
    for k in range(1, subgroup):
        level_ids_copy(k).start()

    @pl.when(sends_right)
    def _():
        own_ids(z + 1).start()

    @pl.when(sends_left)
    def _():
        own_ids(z - 1).start()

    send_own(0)

    def norm_step(p, carry):
        load_piece(p).wait()
        lax.fori_loop(p * per_piece, (p + 1) * per_piece, lambda h, c: (normalize(h), c)[1], 0)
        send_own(p)
        return carry

    lax.fori_loop(1, pieces, norm_step, 0)
    ids_copy.wait()

    def level_forward(p):
        for k in range(1, others):
            arrived = level_piece(peer(subgroup - 2 * k), p, lvl_recv.at[k, p], s)
            arrived.wait_recv()
            level_piece(peer(subgroup - 2 * k), p, mate_recv.at[1], partner).start()

    def relay_step(j):
        block = 1 - jnp.minimum(j // far1, 1)
        chunk = lax.rem(j + near1, chunks)
        hold = relayed(block, chunk, j)
        hold.wait_recv()

        @pl.when(z == pivot)
        def _():
            hold.start()

        @pl.when(z == 1)
        def _():
            returned(block, chunk, across_y).start()
            returned(block, chunk, at(z - 1) | across_y).start()

    crossing = far0 + far1
    stride = chunks // pieces

    def ticks(count, native, lag_relay, lag_level):
        def tick(t, carry):
            native(t)
            j = t - lag_relay

            @pl.when((j >= 0) & (j < crossing))
            def _():
                relay_step(j)

            p = t - lag_level

            @pl.when((p >= 0) & (lax.rem(p, stride) == 0) & (p < pieces * stride))
            def _():
                level_forward(p // stride)

            return carry

        lax.fori_loop(0, count, tick, 0)

    def wait_bulk(index, count):
        bytes_of(count * size, relay_send, bulk_recv.at[index]).wait_recv()

    def spread(i, ids):
        ids_col[i] = jnp.broadcast_to(ids, (LANES, rows)).T

    def wait_home():
        bytes_of(rows, lvl_send, mate_recv.at[0]).wait_recv()
        remote(
            level_ids.at[pl.ds(0, subgroup - 1)], level_ids.at[pl.ds(0, subgroup - 1)],
            ids_send, lid_recv, {"sub": peer(1)},
        ).wait_recv()
        spread(z, level_ids[s])

    def wait_away():
        bytes_of((others - 1) * rows, lvl_send, mate_recv.at[1]).wait_recv()

    def meet(i, low, high, chip, own=False):
        count = high - low
        side = lax.rem(s // 2 + chip, others) * 2
        start = side * rows
        block = level[slot(s), :] if own else foreign[i, low:high, :]
        others_rows = level[pl.ds(pl.multiple_of(start, 2 * rows), 2 * rows), :]
        similar = lax.dot_general(
            block, others_rows, (((1,), (1,)), ((), ())), preferred_element_type=jnp.float32
        )
        own_ids = ids_col[i, low:high, :]
        best = row_part[i, low:high, :]
        for col in range(0, 2 * rows, LANES):
            same = own_ids == level_ids[side + col // rows, :, col % rows : col % rows + LANES]
            if own:
                across = lax.broadcasted_iota(jnp.int32, (rows, LANES), 1) + (col + start)
                down = lax.broadcasted_iota(jnp.int32, (rows, LANES), 0) + s * rows
                same = same & (across != down)
            kept = jnp.where(same, similar[:, col : col + LANES], jnp.float32(-1.0))
            best = jnp.maximum(best, kept)
            if not own:
                columns = jnp.max(kept.reshape(count // SUBLANES, SUBLANES, LANES), axis=0)
                where = pl.ds(pl.multiple_of(start + col, LANES), LANES)
                col_part[:, where] = jnp.maximum(col_part[:, where], columns)
        row_part[i, low:high, :] = best

    def meet_all(i, low, high, own=False):
        for chip in range(others):
            meet(i, low, high, chip, own)

    def flat(i):
        return jnp.max(row_part[i].T, axis=0, keepdims=True)

    def ret_copy(i, owner, where):
        return remote(ret_out.at[i], ret_in.at[owner], ret_send, ret_recv.at[owner], at(where))

    def col_copy(k):
        return remote(col_out.at[peer(k)], col_in.at[s], ret_send, col_recv, {"sub": peer(k)})

    def give(i):
        ret_out[i] = flat(i)
        ret_copy(i, z, i).start()

    half = rows // 2

    @pl.when((z == 0) | (z == last))
    def _():
        lax.fori_loop(0, pieces, lambda p, c: (level_forward(p), c)[1], 0)
        wait_home()
        wait_away()
        meet_all(z, 0, rows, True)

    @pl.when(z == 1)
    def _():
        ids_on(0, z).wait_recv()
        ids_on(0, z + 1).start()

        def native(k):
            @pl.when(k < chunks)
            def _():
                passed_on(0, k, z, first_recv.at[k]).wait_recv()

                @pl.when(k < far0)
                def _():
                    passed_across(k).start()

                @pl.when(k >= far0)
                def _():
                    passed_on(0, k, z + 1, first_recv.at[k]).start()

        ticks(
            max(LAG1[0] + crossing, LAG1[2] + chunks), native,
            LAG1[0] * (1 - rep) + LAG1[1] * rep, LAG1[2] * (1 - rep) + LAG1[3] * rep,
        )
        wait_home()
        wait_away()
        meet_all(z, 0, rows, True)
        spread(0, lane_ids[0])
        meet_all(0, 0, rows)
        give(0)

    @pl.when(z == pivot)
    def _():
        ids_on(1, z).wait_recv()
        ids_on(1, z + 1).start()
        lead = LAG2[4]
        steps = near1 + chunks - far0

        def native(t):
            k = t - lead * rep

            @pl.when((k >= 0) & (k < near1))
            def _():
                passed_on(1, k, z, second_recv.at[k]).wait_recv()
                passed_on(1, k, z + 1, bulk_recv.at[far1_recv]).start()

            m = k - near1 + far0

            @pl.when(k == near1)
            def _():
                ids_on(0, z).wait_recv()
                ids_on(0, z + 1).start()

            @pl.when((k >= near1) & (m < chunks))
            def _():
                passed_on(0, m, z, first_recv.at[m]).wait_recv()

            @pl.when((k >= near1) & (m < chunks // 2))
            def _():
                passed_on(0, m, z + 1, bulk_recv.at[far0a]).start()

            @pl.when((k >= near1) & (m >= chunks // 2) & (m < chunks))
            def _():
                passed_on(0, m, z + 1, bulk_recv.at[far0b]).start()

            @pl.when(k == steps - 9)
            def _():
                wait_home()
                meet(z, 0, rows, 0, True)

            @pl.when(k == steps - 7)
            def _():
                spread(1, lane_ids[1])
                meet(1, 0, half, 0)

            @pl.when(k == steps - 3)
            def _():
                ids_on(last, z).wait_recv()
                spread(last, lane_ids[last])
                wait_bulk(block3, chunks)
                meet(last, 0, rows, 0)

            @pl.when(k == steps - 2)
            def _():
                wait_away()
                for chip in range(1, others):
                    meet(z, 0, rows, chip, True)

            @pl.when(k == steps - 1)
            def _():
                for chip in range(1, others):
                    meet(last, 0, rows, chip)

        ticks(
            steps + lead, native,
            LAG2[0] * (1 - rep) + LAG2[1] * rep, LAG2[2] * (1 - rep) + LAG2[3] * rep,
        )
        spread(0, lane_ids[0])
        wait_bulk(back0, far0)
        meet_all(0, 0, rows)
        give(0)
        wait_bulk(back1, far1)
        for chip in range(1, others):
            meet(1, 0, half, chip)
        meet_all(1, half, rows)
        give(1)
        give(last)

    @pl.when(z == last)
    def _():
        ids_on(1, z).wait_recv()
        spread(1, lane_ids[1])
        ids_on(0, z).wait_recv()
        spread(0, lane_ids[0])
        wait_bulk(far1_recv, near1)
        meet_all(1, 0, half)
        wait_bulk(back1, far1)
        meet_all(1, half, rows)
        give(1)
        wait_bulk(back0, far0)
        wait_bulk(far0a, chunks // 2 - far0)
        meet_all(0, 0, half)
        wait_bulk(far0b, chunks // 2)
        meet_all(0, half, rows)
        give(0)

    @pl.when(z > 0)
    def _():
        for b in range(subgroup):
            col_out[b] = jnp.max(col_part[:, b * rows : (b + 1) * rows], axis=0, keepdims=True)
        for k in range(1, subgroup):
            col_copy(k).start()

    out_ref[...] = flat(z).reshape(rows)

    bytes_of(2 * (others - 1) * rows + rows, lvl_send, col_recv).wait_send()

    def sent_ids(count):
        block = lane_ids.at[pl.ds(0, count)]
        remote(block, block, ids_send, col_recv, {"sub": peer(1)}).wait_send()

    @pl.when((z == 0) | (z == last))
    def _():
        sent_ids(subgroup)

    @pl.when((z > 0) & (z < last))
    def _():
        sent_ids(subgroup + 1)

    @pl.when(z != pivot)
    def _():
        bytes_of(rows, own_send, col_recv).wait_send()

    @pl.when(z == 1)
    def _():
        bytes_of(rows, pass_send, col_recv).wait_send()
        bytes_of(2 * crossing * size, relay_send, col_recv).wait_send()

    @pl.when(z == pivot)
    def _():
        bytes_of((near1 + chunks - far0) * size, pass_send, col_recv).wait_send()
        bytes_of(crossing * size, relay_send, col_recv).wait_send()

    @pl.when(z > 0)
    def _():
        block = col_in.at[pl.ds(0, subgroup - 1)]
        remote(block, block, ret_send, col_recv, {"sub": peer(1)}).wait_recv()
        heard = col_out[s]
        for k in range(1, subgroup):
            heard = jnp.maximum(heard, col_in[peer(k)])
        out_ref[...] = jnp.maximum(out_ref[...], heard.reshape(rows))

    for j in range(1, groups):
        @pl.when((z < j) & (z < pivot) | (z > j) & (z > pivot) & (j >= pivot))
        def _(j=j):
            ret_copy(0, j, z).wait_recv()
            out_ref[...] = jnp.maximum(out_ref[...], ret_in[j].reshape(rows))

    def sent_maxima(count):
        block = col_in.at[pl.ds(0, count)]
        remote(block, block, ret_send, col_recv, {"sub": peer(1)}).wait_send()

    for here, count in ((1, 1), (pivot, 3), (last, 2)):
        @pl.when(z == here)
        def _(count=count):
            sent_maxima(subgroup - 1 + count)


def by_meeting(embeddings, cluster_ids, chunks, pieces):
    rows, features = embeddings.shape
    groups = lax.axis_size("grp")
    subgroup = lax.axis_size("sub")
    dma = pltpu.SemaphoreType.DMA
    return pl.pallas_call(
        functools.partial(meet_kernel, groups, subgroup, chunks, pieces),
        out_shape=pltpu.VMEM((rows,), jnp.float32),
        in_specs=[pl.BlockSpec(memory_space=pl.ANY)] * 2,
        out_specs=pl.BlockSpec(memory_space=pltpu.VMEM),
        scratch_shapes=[
            pltpu.VMEM((rows, features), jnp.bfloat16),
            pltpu.VMEM((subgroup * rows, features), jnp.bfloat16),
            pltpu.VMEM((groups, rows, features), jnp.bfloat16),
            pltpu.VMEM((groups // 2, rows, features), jnp.bfloat16),
            pltpu.VMEM((2 * subgroup, 1, rows), jnp.int32),
            pltpu.VMEM((subgroup, 1, rows), jnp.int32),
            pltpu.VMEM((groups, rows, LANES), jnp.int32),
            pltpu.VMEM((groups, rows, LANES), jnp.float32),
            pltpu.VMEM((SUBLANES, subgroup * rows), jnp.float32),
            pltpu.VMEM((groups, 1, rows), jnp.float32),
            pltpu.VMEM((groups, 1, rows), jnp.float32),
            pltpu.VMEM((subgroup, 1, rows), jnp.float32),
            pltpu.VMEM((2 * subgroup, 1, rows), jnp.float32),
            dma((pieces,)), dma, dma, dma((groups,)), dma,
            dma, dma((subgroup // 2, pieces)), dma((2,)), dma, dma, dma,
            dma((chunks,)), dma((chunks,)), dma((6,)), dma((chunks,)), dma, dma((groups,)), dma,
        ],
        compiler_params=pltpu.CompilerParams(collective_id=0, has_side_effects=True),
    )(embeddings, cluster_ids.reshape(1, rows))


def local(embeddings, cluster_ids):
    rows, features = embeddings.shape
    groups = lax.axis_size("grp")
    subgroup = lax.axis_size("sub")
    held = (groups + subgroup) * rows * features * embeddings.dtype.itemsize
    paired = lax.axis_size("rep") == 2 and subgroup % 2 == 0 and groups == 4
    if held <= VMEM_BUDGET and paired and rows % (LANES * 2) == 0:
        return by_meeting(embeddings, cluster_ids, rows // 16, 4)
    return by_owner(embeddings, cluster_ids)


def solution(mesh):
    return jax.shard_map(
        local,
        mesh=mesh,
        in_specs=(P(("rep", "grp", "sub"), None), P(("rep", "grp", "sub"), None)),
        out_specs=P(("rep", "grp", "sub")),
        check_vma=False,
    )
```

```python
import functools
import math

import jax
import jax.numpy as jnp
from jax import lax
from jax.experimental import pallas as pl
from jax.experimental.pallas import tpu as pltpu
from jax.sharding import PartitionSpec as P

LANES = 128
SUBLANES = 8
VMEM_BUDGET = 24 << 20
MESH = pl.DeviceIdType.MESH


def from_behind(value, axis, by):
    peers = lax.axis_size(axis)
    return lax.ppermute(value, axis, [(i, (i + by) % peers) for i in range(peers)])


def masked_maxima(left_rows, right_rows, right_present, excluded):
    similar = jnp.dot(left_rows, right_rows.T, preferred_element_type=jnp.float32)
    allowed = (right_present[None, :] > 0) & jnp.logical_not(excluded)
    return jnp.where(allowed, similar, jnp.float32(-1.0))


def unit_of(rows, features):
    floats = rows.astype(jnp.float32)
    return (
        floats
        * lax.rsqrt(jnp.mean(floats * floats, axis=1, keepdims=True) + 1e-06)
        / math.sqrt(features)
    ).astype(jnp.bfloat16)


def by_owner(embeddings, cluster_ids):
    rows_dev, features = embeddings.shape
    groups = lax.axis_size("grp")
    subgroup = lax.axis_size("sub")
    capacity = 2 * rows_dev // groups
    unit_rows = unit_of(embeddings, features)
    labels = cluster_ids[:, 0]
    member_table = (labels[:, None] == jnp.arange(groups, dtype=jnp.int32)[None, :]).astype(
        jnp.int32
    )
    running = jnp.cumsum(member_table, axis=0)
    within = jnp.sum(jnp.where(member_table > 0, running - 1, 0), axis=1)
    slot_index = labels * capacity + within
    outgoing = jnp.zeros((groups * capacity, features), jnp.bfloat16).at[slot_index].set(unit_rows)
    occupied = jnp.zeros((groups * capacity,), jnp.int32).at[slot_index].set(1)
    arrived, arrived_present = (
        lax.all_to_all(
            outgoing.reshape(groups, capacity, features),
            "grp",
            split_axis=0,
            concat_axis=0,
            tiled=True,
        ),
        lax.all_to_all(
            occupied.reshape(groups, capacity), "grp", split_axis=0, concat_axis=0, tiled=True
        ),
    )
    owned_rows = arrived.reshape(groups * capacity, features)
    present = arrived_present.reshape(groups * capacity)
    held = owned_rows.shape[0]
    positions = jnp.arange(held, dtype=jnp.int32)
    excluded = positions[:, None] == positions[None, :]
    highest = jnp.max(masked_maxima(owned_rows, owned_rows, present, excluded), axis=1)
    no_exclusion = jnp.zeros((held, held), dtype=bool)
    for offset in range(1, subgroup // 2 + 1):
        peer_rows, peer_present = from_behind((owned_rows, present), "sub", offset)
        scores = masked_maxima(owned_rows, peer_rows, peer_present, no_exclusion)
        highest = jnp.maximum(highest, jnp.max(scores, axis=1))
        if 2 * offset != subgroup:
            column_best = jnp.max(
                jnp.where(present[:, None] > 0, scores, jnp.float32(-1.0)), axis=0
            )
            returned_best = from_behind(column_best, "sub", -offset)
            highest = jnp.maximum(highest, returned_best)
    returned = lax.all_to_all(
        highest.reshape(groups, capacity), "grp", split_axis=0, concat_axis=0, tiled=True
    )
    return returned.reshape(groups * capacity)[slot_index]


LAG1 = (7, 4, 4, 4)
LAG2 = (2, 0, 4, 4, 2)
LEAD = (5, 6)
FAR1 = (7, 9)
EARLY1 = 6


def meet_kernel(
    groups, subgroup, chunks, pieces,
    emb_ref, ids_ref, out_ref,
    emb_in, level, foreign, relay, lane_ids, level_ids, ids_col, row_part, col_part,
    ret_out, ret_in, col_out, col_in,
    in_sem, ids_in, ids_send, ids_recv, lid_recv,
    lvl_send, lvl_recv, mate_recv, own_send, pass_send, relay_send,
    first_recv, second_recv, bulk_recv, relay_recv, ret_send, ret_recv, col_recv,
):
    rows, features = emb_ref.shape
    size = rows // chunks
    load = rows // pieces
    far0 = chunks // 4
    near0 = chunks - far0
    unit = chunks // 16
    early1 = EARLY1 * unit
    pivot = groups // 2
    last = groups - 1
    rep = lax.axis_index("rep")
    depth = lax.axis_index("grp")
    z = depth * (1 - rep) + (last - depth) * rep
    s = lax.axis_index("sub")
    far1 = unit * (FAR1[0] * (1 - rep) + FAR1[1] * rep)
    near1 = chunks - far1
    their_far1 = unit * (FAR1[1] * (1 - rep) + FAR1[0] * rep)
    their_near1 = chunks - their_far1
    partner = s + 1 - 2 * lax.rem(s, 2)
    others = subgroup // 2
    across_y = {"rep": 1 - rep}

    def peer(k):
        return lax.rem(s + k, subgroup)

    def at(where):
        return {"grp": where * (1 - rep) + (last - where) * rep}

    def remote(src, dst, send, recv, where):
        return pltpu.make_async_remote_copy(
            src_ref=src, dst_ref=dst, send_sem=send, recv_sem=recv,
            device_id=where, device_id_type=MESH,
        )

    def slot(b):
        return pl.ds(pl.multiple_of(b * rows, rows), rows)

    def piece(b, p):
        return pl.ds(pl.multiple_of(b * rows + p * load, load), load)

    def own_chunk(k):
        return level.at[pl.ds(pl.multiple_of(s * rows + k * size, size), size), :]

    def part(k):
        return pl.ds(pl.multiple_of(k * size, size), size)

    def load_piece(p):
        where = pl.ds(pl.multiple_of(p * load, load), load)
        return pltpu.make_async_copy(emb_ref.at[where, :], emb_in.at[where, :], in_sem.at[p])

    turn = jnp.where(z == 0, pieces - 1, 0)

    def turned(p):
        return lax.rem(p + turn, pieces)

    for p in range(pieces):
        load_piece(turned(p)).start()
    ids_copy = pltpu.make_async_copy(ids_ref, level_ids.at[s], ids_in)
    ids_copy.start()

    barrier = pltpu.get_barrier_semaphore()
    for k in range(1, subgroup):
        pl.semaphore_signal(barrier, 1, device_id={"sub": peer(k)}, device_id_type=MESH)
    pl.semaphore_signal(barrier, 1, device_id=across_y, device_id_type=MESH)

    @pl.when(z > 0)
    def _():
        pl.semaphore_signal(barrier, 1, device_id=at(z - 1), device_id_type=MESH)

    @pl.when(z < last)
    def _():
        pl.semaphore_signal(barrier, 1, device_id=at(z + 1), device_id_type=MESH)

    @pl.when(z == last)
    def _():
        pl.semaphore_signal(barrier, 1, device_id=at(z - 1) | across_y, device_id_type=MESH)

    col_part[...] = jnp.full(col_part.shape, -1.0, jnp.float32)
    row_part[...] = jnp.full(row_part.shape, -1.0, jnp.float32)

    def level_ids_copy(k):
        return remote(ids_ref, level_ids.at[s], ids_send, lid_recv, {"sub": peer(k)})

    def own_ids(where):
        return remote(ids_ref, lane_ids.at[z], ids_send, ids_recv.at[z], at(where))

    def ids_on(i, where):
        return remote(lane_ids.at[i], lane_ids.at[i], ids_send, ids_recv.at[i], at(where))

    def bytes_of(count, send, recv):
        block = level.at[pl.ds(0, count), :]
        return remote(block, block, send, recv, {"sub": peer(1)})

    back0, back1, far1_recv, far0a, far0b, block3, rest0 = range(7)
    ahead = 3 * chunks // 8
    lead1 = unit * (LEAD[0] * (1 - rep) + LEAD[1] * rep)

    def own_along(k, where, recv):
        return remote(own_chunk(k), foreign.at[z, part(k), :], own_send, recv, at(where))

    def own_across(i, k, j):
        return remote(own_chunk(k), relay.at[i, part(k), :], own_send, relay_recv.at[j], across_y)

    def passed_on(i, k, where, recv):
        block = foreign.at[i, part(k), :]
        return remote(block, block, pass_send, recv, at(where))

    def relayed(i, k, j):
        block = relay.at[i, part(k), :]
        return remote(block, block, relay_send, relay_recv.at[j], at(z - 1))

    def returned(i, k, where):
        return remote(
            relay.at[i, part(k), :], foreign.at[i, part(k), :], relay_send, bulk_recv.at[back0 + i], where
        )

    def level_piece(owner, p, recv, where):
        block = level.at[piece(owner, p), :]
        return remote(block, block, lvl_send, recv, {"sub": where})

    sends_right = z < pivot
    sends_left = z == last

    def start_own(k):
        @pl.when((z == 0) & (k < near0))
        def _():
            own_along(k, z + 1, first_recv.at[k]).start()

        @pl.when((z == 0) & (k >= near0))
        def _():
            own_across(0, k, early1 + k - near0).start()

        @pl.when((z == 1) & (k < lead1))
        def _():
            own_along(k, z + 1, second_recv.at[k]).start()

        @pl.when((z == 1) & (k >= near1))
        def _():
            own_across(1, k, k - near1 + jnp.where(k < near1 + early1, 0, far0)).start()

        @pl.when((z == last) & (k < ahead))
        def _():
            own_along(k, z - 1, bulk_recv.at[block3]).start()

    step = rows // 8
    per_piece = load // step
    per_load = load // size

    def normalize(h):
        where = pl.ds(pl.multiple_of(h * step, step), step)
        into = pl.ds(pl.multiple_of(s * rows + h * step, step), step)
        level[into, :] = unit_of(emb_in[where, :], features)

    def send_own(p):
        @pl.when(z != pivot)
        def _():
            lax.fori_loop(
                per_load * p, per_load * (p + 1), lambda k, c: (start_own(k), c)[1], 0
            )

        for k in range(1, others):
            level_piece(s, p, lvl_recv.at[k - 1, p], peer(2 * k)).start()
        level_piece(s, p, mate_recv.at[0], partner).start()

    load_piece(turn).wait()
    lax.fori_loop(
        turn * per_piece, (turn + 1) * per_piece, lambda h, c: (normalize(h), c)[1], 0
    )
    neighbours = subgroup + sum(c.astype(jnp.int32) for c in (z > 0, z < last, z == 1))
    pl.semaphore_wait(barrier, neighbours)
    for k in range(1, subgroup):
        level_ids_copy(k).start()

    @pl.when(sends_right)
    def _():
        own_ids(z + 1).start()

    @pl.when(sends_left)
    def _():
        own_ids(z - 1).start()

    send_own(turn)

    def norm_step(q, carry):
        p = turned(q)
        load_piece(p).wait()
        lax.fori_loop(p * per_piece, (p + 1) * per_piece, lambda h, c: (normalize(h), c)[1], 0)
        send_own(p)
        return carry

    lax.fori_loop(1, pieces, norm_step, 0)
    ids_copy.wait()

    def level_forward(p):
        for k in range(1, others):
            arrived = level_piece(peer(subgroup - 2 * k), p, lvl_recv.at[k - 1, p], s)
            arrived.wait_recv()
            level_piece(peer(subgroup - 2 * k), p, mate_recv.at[1], partner).start()

    def relay_step(j):
        block = jnp.where((j < early1) | (j >= early1 + far0), 1, 0)
        chunk = j + jnp.where(
            j < early1, their_near1, jnp.where(j < early1 + far0, near0 - early1, their_near1 - far0)
        )
        hold = relayed(block, chunk, j)
        hold.wait_recv()

        @pl.when(z >= pivot)
        def _():
            hold.start()

        @pl.when(z == 1)
        def _():
            returned(block, chunk, across_y).start()
            returned(block, chunk, at(z - 1) | across_y).start()

    crossing = far0 + their_far1
    stride = chunks // pieces

    def ticks(count, native, lag_relay, lag_level):
        def tick(t, carry):
            native(t)
            j = t - lag_relay

            @pl.when((j >= 0) & (j < crossing))
            def _():
                relay_step(j)

            p = t - lag_level

            @pl.when((p >= 0) & (lax.rem(p, stride) == 0) & (p < pieces * stride))
            def _():
                level_forward(p // stride)

            return carry

        lax.fori_loop(0, count, tick, 0)

    def either_way(body):
        for way, far in enumerate(FAR1):
            @pl.when(rep == way)
            def _(far=far):
                body(far * unit)

    def wait_bulk(index, count):
        bytes_of(count * size, relay_send, bulk_recv.at[index]).wait_recv()

    def spread(i, ids):
        ids_col[i] = jnp.broadcast_to(ids, (LANES, rows)).T

    def wait_home():
        bytes_of(rows, lvl_send, mate_recv.at[0]).wait_recv()
        remote(
            level_ids.at[pl.ds(0, subgroup - 1)], level_ids.at[pl.ds(0, subgroup - 1)],
            ids_send, lid_recv, {"sub": peer(1)},
        ).wait_recv()
        spread(z, level_ids[s])

    def wait_away():
        bytes_of((others - 1) * rows, lvl_send, mate_recv.at[1]).wait_recv()

    def meet(i, low, high, chip, own=False):
        count = high - low
        side = lax.rem(s // 2 + chip, others) * 2
        start = side * rows
        block = level[slot(s), :] if own else foreign[i, low:high, :]
        others_rows = level[pl.ds(pl.multiple_of(start, 2 * rows), 2 * rows), :]
        similar = lax.dot_general(
            block, others_rows, (((1,), (1,)), ((), ())), preferred_element_type=jnp.float32
        )
        own_ids = ids_col[i, low:high, :]
        best = row_part[i, low:high, :]
        for col in range(0, 2 * rows, LANES):
            same = own_ids == level_ids[side + col // rows, :, col % rows : col % rows + LANES]
            if own:
                across = lax.broadcasted_iota(jnp.int32, (rows, LANES), 1) + (col + start)
                down = lax.broadcasted_iota(jnp.int32, (rows, LANES), 0) + s * rows
                same = same & (across != down)
            kept = jnp.where(same, similar[:, col : col + LANES], jnp.float32(-1.0))
            best = jnp.maximum(best, kept)
            if not own:
                columns = jnp.max(kept.reshape(count // SUBLANES, SUBLANES, LANES), axis=0)
                where = pl.ds(pl.multiple_of(start + col, LANES), LANES)
                col_part[:, where] = jnp.maximum(col_part[:, where], columns)
        row_part[i, low:high, :] = best

    def meet_all(i, low, high, own=False):
        for chip in range(others):
            meet(i, low, high, chip, own)

    def flat(i):
        return jnp.max(row_part[i].T, axis=0, keepdims=True)

    def ret_copy(i, owner, where):
        return remote(ret_out.at[i], ret_in.at[owner], ret_send, ret_recv.at[owner], at(where))

    def col_copy(k):
        return remote(col_out.at[peer(k)], col_in.at[s], ret_send, col_recv, {"sub": peer(k)})

    def give(i):
        ret_out[i] = flat(i)
        ret_copy(i, z, i).start()

    half = rows // 2

    @pl.when(z == 0)
    def _():
        lax.fori_loop(
            near0, chunks, lambda k, c: (own_along(k, z + 1, bulk_recv.at[rest0]).start(), c)[1], 0
        )

    @pl.when(z == last)
    def _():
        lax.fori_loop(
            early1, early1 + far0, lambda j, c: (relay_step(j), c)[1], 0
        )
        lax.fori_loop(
            ahead, chunks, lambda k, c: (own_along(k, z - 1, bulk_recv.at[block3]).start(), c)[1], 0
        )

    @pl.when((z == 0) | (z == last))
    def _():
        def early(p, carry):
            level_forward(p)

            @pl.when(p == pieces // 2)
            def _():
                wait_home()
                meet(z, 0, rows, 0, True)

            return carry

        lax.fori_loop(0, pieces, early, 0)
        wait_away()
        for chip in range(1, others):
            meet(z, 0, rows, chip, True)

    @pl.when(z == 1)
    def _():
        ids_on(0, z).wait_recv()
        ids_on(0, z + 1).start()

        def native(t):
            @pl.when(t < near0)
            def _():
                passed_on(0, t, z, first_recv.at[t]).wait_recv()
                passed_on(0, t, z + 1, first_recv.at[t]).start()

            @pl.when(t == near0 - 1)
            def _():
                lax.fori_loop(
                    lead1, near1,
                    lambda k, c: (own_along(k, z + 1, second_recv.at[k]).start(), c)[1], 0,
                )

        ticks(
            max(LAG1[0] * unit + far0 + max(FAR1) * unit, (LAG1[2] + 12) * unit + 1), native,
            unit * (LAG1[0] * (1 - rep) + LAG1[1] * rep),
            unit * (LAG1[2] * (1 - rep) + LAG1[3] * rep),
        )
        wait_home()
        wait_away()
        meet_all(z, 0, rows, True)
        spread(0, lane_ids[0])
        wait_bulk(rest0, far0)
        meet_all(0, 0, rows)
        give(0)

    @pl.when(z == pivot)
    def _():
        ids_on(1, z).wait_recv()
        ids_on(1, z + 1).start()
        lead = LAG2[4] * unit
        steps = near1 + near0

        def native(t):
            k = t - lead * rep

            m = k - lead1
            own = k - jnp.where(k < lead1, 0, near0)

            @pl.when((k >= 0) & (k < lead1) | (k >= lead1 + near0) & (k < steps))
            def _():
                passed_on(1, own, z, second_recv.at[own]).wait_recv()
                passed_on(1, own, z + 1, bulk_recv.at[far1_recv]).start()

            @pl.when(m == 0)
            def _():
                ids_on(0, z).wait_recv()
                ids_on(0, z + 1).start()

            @pl.when((m >= 0) & (m < near0))
            def _():
                passed_on(0, m, z, first_recv.at[m]).wait_recv()

            @pl.when((m >= 0) & (m < chunks // 2))
            def _():
                passed_on(0, m, z + 1, bulk_recv.at[far0a]).start()

            @pl.when((m >= chunks // 2) & (m < near0))
            def _():
                passed_on(0, m, z + 1, bulk_recv.at[far0b]).start()

            @pl.when(k == steps - 9 * unit)
            def _():
                wait_home()
                meet(z, 0, rows, 0, True)

            @pl.when(k == steps - 2 * unit)
            def _():
                wait_away()
                for chip in range(1, others):
                    meet(z, 0, rows, chip, True)

        ticks(
            steps + lead, native,
            unit * (LAG2[0] * (1 - rep) + LAG2[1] * rep),
            unit * (LAG2[2] * (1 - rep) + LAG2[3] * rep),
        )
        spread(0, lane_ids[0])
        wait_bulk(back0, far0)
        meet_all(0, 0, rows)
        give(0)
        spread(1, lane_ids[1])
        either_way(lambda far: wait_bulk(back1, far))
        meet_all(1, 0, rows)
        give(1)
        ids_on(last, z).wait_recv()
        spread(last, lane_ids[last])
        wait_bulk(block3, chunks)
        meet_all(last, 0, rows)
        give(last)

    @pl.when(z == last)
    def _():
        ids_on(0, z).wait_recv()
        spread(0, lane_ids[0])
        ids_on(1, z).wait_recv()
        spread(1, lane_ids[1])
        wait_bulk(far0a, chunks // 2)
        meet_all(0, 0, half)
        wait_bulk(far0b, near0 - chunks // 2)
        wait_bulk(back0, far0)
        meet_all(0, half, rows)
        give(0)
        either_way(lambda far: wait_bulk(back1, far))
        either_way(lambda far: wait_bulk(far1_recv, chunks - far))
        meet_all(1, 0, rows)
        give(1)

    @pl.when(z > 0)
    def _():
        for b in range(subgroup):
            col_out[b] = jnp.max(col_part[:, b * rows : (b + 1) * rows], axis=0, keepdims=True)
        for k in range(1, subgroup):
            col_copy(k).start()

    out_ref[...] = flat(z).reshape(rows)

    bytes_of(2 * (others - 1) * rows + rows, lvl_send, col_recv).wait_send()

    def sent_ids(count):
        block = lane_ids.at[pl.ds(0, count)]
        remote(block, block, ids_send, col_recv, {"sub": peer(1)}).wait_send()

    @pl.when((z == 0) | (z == last))
    def _():
        sent_ids(subgroup)

    @pl.when((z > 0) & (z < last))
    def _():
        sent_ids(subgroup + 1)

    @pl.when(z == 0)
    def _():
        bytes_of((chunks + far0) * size, own_send, col_recv).wait_send()

    @pl.when((z == 1) | (z == last))
    def _():
        bytes_of(rows, own_send, col_recv).wait_send()

    @pl.when(z == last)
    def _():
        bytes_of(far0 * size, relay_send, col_recv).wait_send()

    @pl.when(z == 1)
    def _():
        bytes_of((chunks - far0) * size, pass_send, col_recv).wait_send()
        either_way(
            lambda far: bytes_of(
                2 * (far0 + sum(FAR1) * unit - far) * size, relay_send, col_recv
            ).wait_send()
        )

    @pl.when(z == pivot)
    def _():
        either_way(
            lambda far: bytes_of((chunks - far + near0) * size, pass_send, col_recv).wait_send()
        )
        either_way(
            lambda far: bytes_of(
                (far0 + sum(FAR1) * unit - far) * size, relay_send, col_recv
            ).wait_send()
        )

    @pl.when(z > 0)
    def _():
        block = col_in.at[pl.ds(0, subgroup - 1)]
        remote(block, block, ret_send, col_recv, {"sub": peer(1)}).wait_recv()
        heard = col_out[s]
        for k in range(1, subgroup):
            heard = jnp.maximum(heard, col_in[peer(k)])
        out_ref[...] = jnp.maximum(out_ref[...], heard.reshape(rows))

    for j in range(1, groups):
        @pl.when((z < j) & (z < pivot) | (z > j) & (z > pivot) & (j >= pivot))
        def _(j=j):
            ret_copy(0, j, z).wait_recv()
            out_ref[...] = jnp.maximum(out_ref[...], ret_in[j].reshape(rows))

    def sent_maxima(count):
        block = col_in.at[pl.ds(0, count)]
        remote(block, block, ret_send, col_recv, {"sub": peer(1)}).wait_send()

    for here, count in ((1, 1), (pivot, 3), (last, 2)):
        @pl.when(z == here)
        def _(count=count):
            sent_maxima(subgroup - 1 + count)


def by_meeting(embeddings, cluster_ids, chunks, pieces):
    rows, features = embeddings.shape
    groups = lax.axis_size("grp")
    subgroup = lax.axis_size("sub")
    dma = pltpu.SemaphoreType.DMA
    return pl.pallas_call(
        functools.partial(meet_kernel, groups, subgroup, chunks, pieces),
        out_shape=pltpu.VMEM((rows,), jnp.float32),
        in_specs=[pl.BlockSpec(memory_space=pl.ANY)] * 2,
        out_specs=pl.BlockSpec(memory_space=pltpu.VMEM),
        scratch_shapes=[
            pltpu.VMEM((rows, features), jnp.bfloat16),
            pltpu.VMEM((subgroup * rows, features), jnp.bfloat16),
            pltpu.VMEM((groups, rows, features), jnp.bfloat16),
            pltpu.VMEM((groups // 2, rows, features), jnp.bfloat16),
            pltpu.VMEM((2 * subgroup, 1, rows), jnp.int32),
            pltpu.VMEM((subgroup, 1, rows), jnp.int32),
            pltpu.VMEM((groups, rows, LANES), jnp.int32),
            pltpu.VMEM((groups, rows, LANES), jnp.float32),
            pltpu.VMEM((SUBLANES, subgroup * rows), jnp.float32),
            pltpu.VMEM((groups, 1, rows), jnp.float32),
            pltpu.VMEM((groups, 1, rows), jnp.float32),
            pltpu.VMEM((subgroup, 1, rows), jnp.float32),
            pltpu.VMEM((2 * subgroup, 1, rows), jnp.float32),
            dma((pieces,)), dma, dma, dma((groups,)), dma,
            dma, dma((max(subgroup // 2 - 1, 1), pieces)), dma((2,)), dma, dma, dma,
            dma((3 * chunks // 4,)), dma((chunks - min(FAR1) * chunks // 16,)), dma((7,)),
            dma((chunks // 4 + max(FAR1) * chunks // 16,)),
            dma, dma((groups,)), dma,
        ],
        compiler_params=pltpu.CompilerParams(collective_id=0, has_side_effects=True),
    )(embeddings, cluster_ids.reshape(1, rows))


def local(embeddings, cluster_ids):
    rows, features = embeddings.shape
    groups = lax.axis_size("grp")
    subgroup = lax.axis_size("sub")
    held = (groups + subgroup) * rows * features * embeddings.dtype.itemsize
    paired = lax.axis_size("rep") == 2 and subgroup % 2 == 0 and groups == 4
    if held <= VMEM_BUDGET and paired and rows % (LANES * 2) == 0:
        return by_meeting(embeddings, cluster_ids, rows // 16, 4)
    return by_owner(embeddings, cluster_ids)


def solution(mesh):
    return jax.shard_map(
        local,
        mesh=mesh,
        in_specs=(P(("rep", "grp", "sub"), None), P(("rep", "grp", "sub"), None)),
        out_specs=P(("rep", "grp", "sub")),
        check_vma=False,
    )
```

```python
import functools
import math

import jax
import jax.numpy as jnp
from jax import lax
from jax.experimental import pallas as pl
from jax.experimental.pallas import tpu as pltpu
from jax.sharding import PartitionSpec as P

LANES = 128
SUBLANES = 8
VMEM_BUDGET = 24 << 20
MESH = pl.DeviceIdType.MESH


def from_behind(value, axis, by):
    peers = lax.axis_size(axis)
    return lax.ppermute(value, axis, [(i, (i + by) % peers) for i in range(peers)])


def masked_maxima(left_rows, right_rows, right_present, excluded):
    similar = jnp.dot(left_rows, right_rows.T, preferred_element_type=jnp.float32)
    allowed = (right_present[None, :] > 0) & jnp.logical_not(excluded)
    return jnp.where(allowed, similar, jnp.float32(-1.0))


def unit_of(rows, features):
    floats = rows.astype(jnp.float32)
    return (
        floats
        * lax.rsqrt(jnp.mean(floats * floats, axis=1, keepdims=True) + 1e-06)
        / math.sqrt(features)
    ).astype(jnp.bfloat16)


def by_owner(embeddings, cluster_ids):
    rows_dev, features = embeddings.shape
    groups = lax.axis_size("grp")
    subgroup = lax.axis_size("sub")
    capacity = 2 * rows_dev // groups
    unit_rows = unit_of(embeddings, features)
    labels = cluster_ids[:, 0]
    member_table = (labels[:, None] == jnp.arange(groups, dtype=jnp.int32)[None, :]).astype(
        jnp.int32
    )
    running = jnp.cumsum(member_table, axis=0)
    within = jnp.sum(jnp.where(member_table > 0, running - 1, 0), axis=1)
    slot_index = labels * capacity + within
    outgoing = jnp.zeros((groups * capacity, features), jnp.bfloat16).at[slot_index].set(unit_rows)
    occupied = jnp.zeros((groups * capacity,), jnp.int32).at[slot_index].set(1)
    arrived, arrived_present = (
        lax.all_to_all(
            outgoing.reshape(groups, capacity, features),
            "grp",
            split_axis=0,
            concat_axis=0,
            tiled=True,
        ),
        lax.all_to_all(
            occupied.reshape(groups, capacity), "grp", split_axis=0, concat_axis=0, tiled=True
        ),
    )
    owned_rows = arrived.reshape(groups * capacity, features)
    present = arrived_present.reshape(groups * capacity)
    held = owned_rows.shape[0]
    positions = jnp.arange(held, dtype=jnp.int32)
    excluded = positions[:, None] == positions[None, :]
    highest = jnp.max(masked_maxima(owned_rows, owned_rows, present, excluded), axis=1)
    no_exclusion = jnp.zeros((held, held), dtype=bool)
    for offset in range(1, subgroup // 2 + 1):
        peer_rows, peer_present = from_behind((owned_rows, present), "sub", offset)
        scores = masked_maxima(owned_rows, peer_rows, peer_present, no_exclusion)
        highest = jnp.maximum(highest, jnp.max(scores, axis=1))
        if 2 * offset != subgroup:
            column_best = jnp.max(
                jnp.where(present[:, None] > 0, scores, jnp.float32(-1.0)), axis=0
            )
            returned_best = from_behind(column_best, "sub", -offset)
            highest = jnp.maximum(highest, returned_best)
    returned = lax.all_to_all(
        highest.reshape(groups, capacity), "grp", split_axis=0, concat_axis=0, tiled=True
    )
    return returned.reshape(groups * capacity)[slot_index]


LAG1 = (7, 4, 4, 4)
LAG2 = (1, 0, 4, 4, 2)
REST0 = 1
HOME = (5, 9)
LEAD = (3, 7)
FAR1 = (7, 9)
EARLY1 = (4, 6)
AHEAD = (6, 4)
SKIP = 1


def meet_kernel(
    groups, subgroup, chunks, pieces,
    emb_ref, ids_ref, out_ref,
    emb_in, level, foreign, relay, lane_ids, level_ids, ids_col, row_part, col_part,
    ret_out, ret_in, col_out, col_in,
    in_sem, ids_in, ids_send, ids_recv, lid_recv,
    lvl_send, lvl_recv, mate_recv, own_send, pass_send, relay_send,
    first_recv, second_recv, bulk_recv, relay_recv, ret_send, ret_recv, col_recv,
):
    rows, features = emb_ref.shape
    size = rows // chunks
    load = rows // pieces
    far0 = chunks // 4
    near0 = chunks - far0
    unit = chunks // 16
    skip = SKIP * unit
    pivot = groups // 2
    last = groups - 1
    rep = lax.axis_index("rep")
    depth = lax.axis_index("grp")
    z = depth * (1 - rep) + (last - depth) * rep
    s = lax.axis_index("sub")
    far1 = unit * (FAR1[0] * (1 - rep) + FAR1[1] * rep)
    near1 = chunks - far1
    their_far1 = unit * (FAR1[1] * (1 - rep) + FAR1[0] * rep)
    their_near1 = chunks - their_far1
    early1 = unit * (EARLY1[0] * (1 - rep) + EARLY1[1] * rep)
    their_early1 = unit * (EARLY1[1] * (1 - rep) + EARLY1[0] * rep)
    partner = s + 1 - 2 * lax.rem(s, 2)
    others = subgroup // 2
    across_y = {"rep": 1 - rep}

    def peer(k):
        return lax.rem(s + k, subgroup)

    def at(where):
        return {"grp": where * (1 - rep) + (last - where) * rep}

    def remote(src, dst, send, recv, where):
        return pltpu.make_async_remote_copy(
            src_ref=src, dst_ref=dst, send_sem=send, recv_sem=recv,
            device_id=where, device_id_type=MESH,
        )

    def slot(b):
        return pl.ds(pl.multiple_of(b * rows, rows), rows)

    def piece(b, p):
        return pl.ds(pl.multiple_of(b * rows + p * load, load), load)

    def own_chunk(k):
        return level.at[pl.ds(pl.multiple_of(s * rows + k * size, size), size), :]

    def part(k):
        return pl.ds(pl.multiple_of(k * size, size), size)

    def load_piece(p):
        where = pl.ds(pl.multiple_of(p * load, load), load)
        return pltpu.make_async_copy(emb_ref.at[where, :], emb_in.at[where, :], in_sem.at[p])

    turn = jnp.where(z == 0, pieces - 1, 0)

    def turned(p):
        return lax.rem(p + turn, pieces)

    for p in range(pieces):
        load_piece(turned(p)).start()
    ids_copy = pltpu.make_async_copy(ids_ref, level_ids.at[s], ids_in)
    ids_copy.start()

    barrier = pltpu.get_barrier_semaphore()
    for k in range(1, subgroup):
        pl.semaphore_signal(barrier, 1, device_id={"sub": peer(k)}, device_id_type=MESH)
    pl.semaphore_signal(barrier, 1, device_id=across_y, device_id_type=MESH)

    @pl.when(z > 0)
    def _():
        pl.semaphore_signal(barrier, 1, device_id=at(z - 1), device_id_type=MESH)

    @pl.when(z < last)
    def _():
        pl.semaphore_signal(barrier, 1, device_id=at(z + 1), device_id_type=MESH)

    @pl.when(z == last)
    def _():
        pl.semaphore_signal(barrier, 1, device_id=at(z - 1) | across_y, device_id_type=MESH)

    col_part[...] = jnp.full(col_part.shape, -1.0, jnp.float32)
    row_part[...] = jnp.full(row_part.shape, -1.0, jnp.float32)

    def level_ids_copy(k):
        return remote(ids_ref, level_ids.at[s], ids_send, lid_recv, {"sub": peer(k)})

    def own_ids(where):
        return remote(ids_ref, lane_ids.at[z], ids_send, ids_recv.at[z], at(where))

    def ids_on(i, where):
        return remote(lane_ids.at[i], lane_ids.at[i], ids_send, ids_recv.at[i], at(where))

    def bytes_of(count, send, recv):
        block = level.at[pl.ds(0, count), :]
        return remote(block, block, send, recv, {"sub": peer(1)})

    back0, back1, block3 = range(3)
    far1_recv, far0a, far0b, rest0 = range(4)
    ahead = unit * (AHEAD[0] * (1 - rep) + AHEAD[1] * rep)
    lead1 = unit * (LEAD[0] * (1 - rep) + LEAD[1] * rep)

    def own_along(k, where, recv):
        return remote(own_chunk(k), foreign.at[z, part(k), :], own_send, recv, at(where))

    def own_across(i, k, j):
        return remote(own_chunk(k), relay.at[i, part(k), :], own_send, relay_recv.at[j], across_y)

    def passed_on(i, k, where, recv):
        block = foreign.at[i, part(k), :]
        return remote(block, block, pass_send, recv, at(where))

    def relayed(i, k, j):
        block = relay.at[i, part(k), :]
        return remote(block, block, relay_send, relay_recv.at[j], at(z - 1))

    def returned(i, k, where):
        return remote(
            relay.at[i, part(k), :], foreign.at[i, part(k), :], relay_send, bulk_recv.at[back0 + i], where
        )

    def level_piece(owner, p, recv, where):
        block = level.at[piece(owner, p), :]
        return remote(block, block, lvl_send, recv, {"sub": where})

    sends_right = z < pivot
    sends_left = z == last

    def start_own(k):
        @pl.when((z == 0) & (k < near0))
        def _():
            own_along(k, z + 1, first_recv.at[k]).start()

        @pl.when((z == 0) & (k >= near0))
        def _():
            own_across(0, k, early1 + k - near0).start()

        @pl.when((z == 1) & (k < lead1))
        def _():
            own_along(k, z + 1, second_recv.at[k]).start()

        @pl.when((z == 1) & (k >= near1))
        def _():
            own_across(1, k, k - near1 + jnp.where(k < near1 + early1, 0, far0)).start()

        @pl.when((z == last) & (k < ahead))
        def _():
            own_along(k, z - 1, bulk_recv.at[block3]).start()

    step = rows // 8
    per_piece = load // step
    per_load = load // size

    def normalize(h):
        where = pl.ds(pl.multiple_of(h * step, step), step)
        into = pl.ds(pl.multiple_of(s * rows + h * step, step), step)
        level[into, :] = unit_of(emb_in[where, :], features)

    def send_own(p):
        @pl.when(z != pivot)
        def _():
            lax.fori_loop(
                per_load * p, per_load * (p + 1), lambda k, c: (start_own(k), c)[1], 0
            )

        for k in range(1, others):
            level_piece(s, p, lvl_recv.at[k - 1, p], peer(2 * k)).start()
        level_piece(s, p, mate_recv.at[0], partner).start()

    load_piece(turn).wait()
    lax.fori_loop(
        turn * per_piece, (turn + 1) * per_piece, lambda h, c: (normalize(h), c)[1], 0
    )
    neighbours = subgroup + sum(c.astype(jnp.int32) for c in (z > 0, z < last, z == 1))
    pl.semaphore_wait(barrier, neighbours)
    for k in range(1, subgroup):
        level_ids_copy(k).start()

    @pl.when(sends_right)
    def _():
        own_ids(z + 1).start()

    @pl.when(sends_left)
    def _():
        own_ids(z - 1).start()

    send_own(turn)

    def norm_step(q, carry):
        p = turned(q)
        load_piece(p).wait()
        lax.fori_loop(p * per_piece, (p + 1) * per_piece, lambda h, c: (normalize(h), c)[1], 0)
        send_own(p)
        return carry

    lax.fori_loop(1, pieces, norm_step, 0)
    ids_copy.wait()

    def level_forward(p):
        for k in range(1, others):
            arrived = level_piece(peer(subgroup - 2 * k), p, lvl_recv.at[k - 1, p], s)
            arrived.wait_recv()
            level_piece(peer(subgroup - 2 * k), p, mate_recv.at[1], partner).start()

    def relay_step(j):
        block = jnp.where((j < their_early1) | (j >= their_early1 + far0), 1, 0)
        chunk = j + jnp.where(
            j < their_early1, their_near1, jnp.where(j < their_early1 + far0, near0 - their_early1, their_near1 - far0)
        )
        hold = relayed(block, chunk, j)
        hold.wait_recv()

        @pl.when(z >= pivot)
        def _():
            hold.start()

        @pl.when(z == 1)
        def _():
            returned(block, chunk, across_y).start()
            returned(block, chunk, at(z - 1) | across_y).start()

    crossing = far0 + their_far1
    stride = chunks // pieces

    def ticks(count, native, lag_relay, lag_level):
        def tick(t, carry):
            native(t)
            j = t - lag_relay

            @pl.when((j >= 0) & (j < crossing))
            def _():
                relay_step(j)

            p = t - lag_level

            @pl.when((p >= 0) & (lax.rem(p, stride) == 0) & (p < pieces * stride))
            def _():
                level_forward(p // stride)

            return carry

        lax.fori_loop(0, count, tick, 0)

    def either_way(body):
        for way, far in enumerate(FAR1):
            @pl.when(rep == way)
            def _(far=far):
                body(far * unit)

    def wait_bulk(index, count, among=bulk_recv):
        bytes_of(count * size, relay_send, among.at[index]).wait_recv()

    def spread(i, ids):
        ids_col[i] = jnp.broadcast_to(ids, (LANES, rows)).T

    def wait_home():
        bytes_of(rows, lvl_send, mate_recv.at[0]).wait_recv()
        remote(
            level_ids.at[pl.ds(0, subgroup - 1)], level_ids.at[pl.ds(0, subgroup - 1)],
            ids_send, lid_recv, {"sub": peer(1)},
        ).wait_recv()
        spread(z, level_ids[s])

    def wait_away():
        bytes_of((others - 1) * rows, lvl_send, mate_recv.at[1]).wait_recv()

    def meet(i, low, high, chip, own=False):
        meet_rows(((i, low, high),), chip, own)

    def meet_rows(parts, chip, own=False):
        side = lax.rem(s // 2 + chip, others) * 2
        start = side * rows
        if own:
            block = level[slot(s), :]
        else:
            block = jnp.concatenate([foreign[i, low:high, :] for i, low, high in parts], axis=0)
        others_rows = level[pl.ds(pl.multiple_of(start, 2 * rows), 2 * rows), :]
        similar = lax.dot_general(
            block, others_rows, (((1,), (1,)), ((), ())), preferred_element_type=jnp.float32
        )
        top = 0
        for i, low, high in parts:
            count = high - low
            own_ids = ids_col[i, low:high, :]
            best = row_part[i, low:high, :]
            for col in range(0, 2 * rows, LANES):
                same = own_ids == level_ids[side + col // rows, :, col % rows : col % rows + LANES]
                if own:
                    across = lax.broadcasted_iota(jnp.int32, (rows, LANES), 1) + (col + start)
                    down = lax.broadcasted_iota(jnp.int32, (rows, LANES), 0) + s * rows
                    same = same & (across != down)
                kept = jnp.where(
                    same, similar[top : top + count, col : col + LANES], jnp.float32(-1.0)
                )
                best = jnp.maximum(best, kept)
                if not own:
                    columns = jnp.max(kept.reshape(count // SUBLANES, SUBLANES, LANES), axis=0)
                    where = pl.ds(pl.multiple_of(start + col, LANES), LANES)
                    col_part[:, where] = jnp.maximum(col_part[:, where], columns)
            row_part[i, low:high, :] = best
            top += count

    def meet_all(i, low, high, own=False):
        for chip in range(others):
            meet(i, low, high, chip, own)

    def flat(i):
        return jnp.max(row_part[i].T, axis=0, keepdims=True)

    def ret_copy(i, owner, where):
        return remote(ret_out.at[i], ret_in.at[owner], ret_send, ret_recv.at[owner], at(where))

    def columns_of(b):
        where = pl.ds(pl.multiple_of(b * rows, rows), rows)
        return jnp.max(col_part[:, where], axis=0, keepdims=True)

    def send_columns(b):
        col_out[b] = columns_of(b)
        remote(col_out.at[b], col_in.at[s], ret_send, col_recv, {"sub": b}).start()

    def give(i):
        ret_out[i] = flat(i)
        ret_copy(i, z, i).start()

    def finish(parts, blocks):
        for chip in range(1, others):
            meet_rows(parts, chip)
            for b in range(2):
                send_columns(lax.rem(s // 2 + chip, others) * 2 + b)
        meet_rows(parts, 0)
        for i in blocks:
            give(i)
        send_columns(partner)

    half = rows // 2

    @pl.when(z == last)
    def _():
        lax.fori_loop(
            their_early1, their_early1 + far0, lambda j, c: (relay_step(j), c)[1], 0
        )
        lax.fori_loop(
            ahead, chunks, lambda k, c: (own_along(k, z - 1, bulk_recv.at[block3]).start(), c)[1], 0
        )

    @pl.when((z == 0) | (z == last))
    def _():
        def early(p, carry):
            level_forward(p)

            @pl.when((z == 0) & (p == REST0))
            def _():
                lax.fori_loop(
                    near0, chunks,
                    lambda k, c: (own_along(k, z + 1, second_recv.at[rest0]).start(), c)[1], 0,
                )

            @pl.when(p == pieces // 2)
            def _():
                wait_home()
                meet(z, 0, rows, 0, True)

            return carry

        lax.fori_loop(0, pieces, early, 0)
        wait_away()
        for chip in range(1, others):
            meet(z, 0, rows, chip, True)

    @pl.when(z == 1)
    def _():
        ids_on(0, z).wait_recv()
        ids_on(0, z + 1).start()

        def native(t):
            @pl.when(t < near0)
            def _():
                passed_on(0, t, z, first_recv.at[t]).wait_recv()

                @pl.when((rep == 1) & (t >= near0 - skip))
                def _():
                    passed_on(0, t, z + 2, second_recv.at[far0b]).start()

                passed_on(0, t, z + 1, first_recv.at[t]).start()

            @pl.when(t == near0 - 1)
            def _():
                def late(k, carry):
                    @pl.when((rep == 0) & (k >= near1 - skip))
                    def _():
                        own_along(k, z + 2, second_recv.at[far1_recv]).start()

                    own_along(k, z + 1, second_recv.at[k]).start()
                    return carry

                lax.fori_loop(lead1, near1, late, 0)

        ticks(
            max(LAG1[0] * unit + far0 + max(FAR1) * unit, (LAG1[2] + 12) * unit + 1), native,
            unit * (LAG1[0] * (1 - rep) + LAG1[1] * rep),
            unit * (LAG1[2] * (1 - rep) + LAG1[3] * rep),
        )
        wait_home()
        wait_away()
        spread(0, lane_ids[0])
        wait_bulk(rest0, far0, second_recv)
        finish(((0, 0, rows),), (0,))
        meet_all(z, 0, rows, True)

    @pl.when(z == pivot)
    def _():
        ids_on(1, z).wait_recv()
        ids_on(1, z + 1).start()
        lead = LAG2[4] * unit

        def meet_first():
            spread(0, lane_ids[0])
            wait_bulk(back0, far0)
            meet_all(0, 0, rows)
            give(0)

        def own_away():
            for chip in range(1, others):
                meet(z, 0, rows, chip, True)

        steps = near1 + near0

        def native(t):
            k = t - lead * rep

            m = k - lead1
            own = k - jnp.where(k < lead1, 0, near0)

            @pl.when((k >= 0) & (k < lead1) | (k >= lead1 + near0) & (k < steps))
            def _():
                passed_on(1, own, z, second_recv.at[own]).wait_recv()

                @pl.when((rep == 1) | (own < near1 - skip))
                def _():
                    passed_on(1, own, z + 1, second_recv.at[far1_recv]).start()

            @pl.when(m == 0)
            def _():
                ids_on(0, z).wait_recv()
                ids_on(0, z + 1).start()

            @pl.when((m >= 0) & (m < near0))
            def _():
                passed_on(0, m, z, first_recv.at[m]).wait_recv()

            @pl.when((m >= 0) & (m < chunks // 2))
            def _():
                passed_on(0, m, z + 1, second_recv.at[far0a]).start()

            @pl.when((m >= chunks // 2) & (m < near0 - skip * rep))
            def _():
                passed_on(0, m, z + 1, second_recv.at[far0b]).start()

            @pl.when(k == steps - unit * (HOME[0] * (1 - rep) + HOME[1] * rep))
            def _():
                wait_home()
                meet(z, 0, rows, 0, True)

            @pl.when((k == steps - 2 * unit) & (rep == 0))
            def _():
                wait_away()
                meet_first()

            @pl.when((k == steps - 2 * unit) & (rep == 1))
            def _():
                wait_away()
                own_away()

        ticks(
            steps + lead, native,
            unit * (LAG2[0] * (1 - rep) + LAG2[1] * rep),
            unit * (LAG2[2] * (1 - rep) + LAG2[3] * rep),
        )
        def await_last():
            ids_on(last, z).wait_recv()
            spread(last, lane_ids[last])
            wait_bulk(block3, chunks)

        @pl.when(rep == 1)
        def _():
            await_last()
            meet_all(last, 0, rows)
            give(last)
            meet_first()

        spread(1, lane_ids[1])
        either_way(lambda far: wait_bulk(back1, far))

        @pl.when(rep == 0)
        def _():
            meet_all(1, 0, rows)
            give(1)
            await_last()
            finish(((last, 0, rows),), (last,))
            own_away()

        @pl.when(rep == 1)
        def _():
            finish(((1, 0, rows),), (1,))

    @pl.when(z == last)
    def _():
        ids_on(0, z).wait_recv()
        spread(0, lane_ids[0])
        ids_on(1, z).wait_recv()
        spread(1, lane_ids[1])

        def first_half():
            wait_bulk(far0a, chunks // 2, second_recv)
            meet_all(0, 0, half)

        def await_second_half():
            wait_bulk(far0b, near0 - chunks // 2, second_recv)
            wait_bulk(back0, far0)

        @pl.when(rep == 0)
        def _():
            first_half()
            await_second_half()
            meet_all(0, half, rows)
            give(0)
            wait_bulk(back1, FAR1[0] * unit)
            wait_bulk(far1_recv, chunks - FAR1[0] * unit, second_recv)
            meet_all(1, 0, rows)
            give(1)
            for k in range(1, subgroup):
                send_columns(peer(k))

        @pl.when(rep == 1)
        def _():
            near = chunks - FAR1[1] * unit
            wait_bulk(far1_recv, near, second_recv)
            meet_all(1, 0, near * size)
            first_half()
            await_second_half()
            wait_bulk(back1, FAR1[1] * unit)
            finish(((0, half, rows), (1, near * size, rows)), (1, 0))

    out_ref[...] = flat(z).reshape(rows)

    bytes_of(2 * (others - 1) * rows + rows, lvl_send, col_recv).wait_send()

    def sent_ids(count):
        block = lane_ids.at[pl.ds(0, count)]
        remote(block, block, ids_send, col_recv, {"sub": peer(1)}).wait_send()

    @pl.when((z == 0) | (z == last))
    def _():
        sent_ids(subgroup)

    @pl.when((z > 0) & (z < last))
    def _():
        sent_ids(subgroup + 1)

    @pl.when(z == 0)
    def _():
        bytes_of((chunks + far0) * size, own_send, col_recv).wait_send()

    @pl.when(z == 1)
    def _():
        for way in (0, 1):
            @pl.when(rep == way)
            def _(way=way):
                bytes_of((chunks + skip * (1 - way)) * size, own_send, col_recv).wait_send()
                bytes_of((near0 + skip * way) * size, pass_send, col_recv).wait_send()

    @pl.when(z == last)
    def _():
        bytes_of(rows, own_send, col_recv).wait_send()
        bytes_of(far0 * size, relay_send, col_recv).wait_send()

    @pl.when(z == 1)
    def _():
        either_way(
            lambda far: bytes_of(
                2 * (far0 + sum(FAR1) * unit - far) * size, relay_send, col_recv
            ).wait_send()
        )

    @pl.when(z == pivot)
    def _():
        either_way(
            lambda far: bytes_of((chunks - far - skip + near0) * size, pass_send, col_recv).wait_send()
        )
        either_way(
            lambda far: bytes_of(
                (far0 + sum(FAR1) * unit - far) * size, relay_send, col_recv
            ).wait_send()
        )

    @pl.when(z > 0)
    def _():
        block = col_in.at[pl.ds(0, subgroup - 1)]
        remote(block, block, ret_send, col_recv, {"sub": peer(1)}).wait_recv()
        heard = columns_of(s)
        for k in range(1, subgroup):
            heard = jnp.maximum(heard, col_in[peer(k)])
        out_ref[...] = jnp.maximum(out_ref[...], heard.reshape(rows))

    for j in range(1, groups):
        @pl.when((z < j) & (z < pivot) | (z > j) & (z > pivot) & (j >= pivot))
        def _(j=j):
            ret_copy(0, j, z).wait_recv()
            out_ref[...] = jnp.maximum(out_ref[...], ret_in[j].reshape(rows))

    def sent_maxima(count):
        block = col_in.at[pl.ds(0, count)]
        remote(block, block, ret_send, col_recv, {"sub": peer(1)}).wait_send()

    for here, count in ((1, 1), (pivot, 3), (last, 2)):
        @pl.when(z == here)
        def _(count=count):
            sent_maxima(subgroup - 1 + count)


def by_meeting(embeddings, cluster_ids, chunks, pieces):
    rows, features = embeddings.shape
    groups = lax.axis_size("grp")
    subgroup = lax.axis_size("sub")
    dma = pltpu.SemaphoreType.DMA
    return pl.pallas_call(
        functools.partial(meet_kernel, groups, subgroup, chunks, pieces),
        out_shape=pltpu.VMEM((rows,), jnp.float32),
        in_specs=[pl.BlockSpec(memory_space=pl.ANY)] * 2,
        out_specs=pl.BlockSpec(memory_space=pltpu.VMEM),
        scratch_shapes=[
            pltpu.VMEM((rows, features), jnp.bfloat16),
            pltpu.VMEM((subgroup * rows, features), jnp.bfloat16),
            pltpu.VMEM((groups, rows, features), jnp.bfloat16),
            pltpu.VMEM((groups // 2, rows, features), jnp.bfloat16),
            pltpu.VMEM((2 * subgroup, 1, rows), jnp.int32),
            pltpu.VMEM((subgroup, 1, rows), jnp.int32),
            pltpu.VMEM((groups, rows, LANES), jnp.int32),
            pltpu.VMEM((groups, rows, LANES), jnp.float32),
            pltpu.VMEM((SUBLANES, subgroup * rows), jnp.float32),
            pltpu.VMEM((groups, 1, rows), jnp.float32),
            pltpu.VMEM((groups, 1, rows), jnp.float32),
            pltpu.VMEM((subgroup, 1, rows), jnp.float32),
            pltpu.VMEM((2 * subgroup, 1, rows), jnp.float32),
            dma((pieces,)), dma, dma, dma((groups,)), dma,
            dma, dma((max(subgroup // 2 - 1, 1), pieces)), dma((2,)), dma, dma, dma,
            dma((3 * chunks // 4,)), dma((chunks - min(FAR1) * chunks // 16,)), dma((3,)),
            dma((chunks // 4 + max(FAR1) * chunks // 16,)),
            dma, dma((groups,)), dma,
        ],
        compiler_params=pltpu.CompilerParams(collective_id=0, has_side_effects=True),
    )(embeddings, cluster_ids.reshape(1, rows))


def local(embeddings, cluster_ids):
    rows, features = embeddings.shape
    groups = lax.axis_size("grp")
    subgroup = lax.axis_size("sub")
    held = (groups + subgroup) * rows * features * embeddings.dtype.itemsize
    paired = lax.axis_size("rep") == 2 and subgroup % 2 == 0 and groups == 4
    if held <= VMEM_BUDGET and paired and rows % (LANES * 2) == 0:
        return by_meeting(embeddings, cluster_ids, rows // 16, 4)
    return by_owner(embeddings, cluster_ids)


def solution(mesh):
    return jax.shard_map(
        local,
        mesh=mesh,
        in_specs=(P(("rep", "grp", "sub"), None), P(("rep", "grp", "sub"), None)),
        out_specs=P(("rep", "grp", "sub")),
        check_vma=False,
    )
```

```python
import functools
import math

import jax
import jax.numpy as jnp
from jax import lax
from jax.experimental import pallas as pl
from jax.experimental.pallas import tpu as pltpu
from jax.sharding import PartitionSpec as P

LANES = 128
SUBLANES = 8
VMEM_BUDGET = 24 << 20
MESH = pl.DeviceIdType.MESH


def from_behind(value, axis, by):
    peers = lax.axis_size(axis)
    return lax.ppermute(value, axis, [(i, (i + by) % peers) for i in range(peers)])


def masked_maxima(left_rows, right_rows, right_present, excluded):
    similar = jnp.dot(left_rows, right_rows.T, preferred_element_type=jnp.float32)
    allowed = (right_present[None, :] > 0) & jnp.logical_not(excluded)
    return jnp.where(allowed, similar, jnp.float32(-1.0))


def unit_of(rows, features):
    floats = rows.astype(jnp.float32)
    return (
        floats
        * lax.rsqrt(jnp.mean(floats * floats, axis=1, keepdims=True) + 1e-06)
        / math.sqrt(features)
    ).astype(jnp.bfloat16)


def by_owner(embeddings, cluster_ids):
    rows_dev, features = embeddings.shape
    groups = lax.axis_size("grp")
    subgroup = lax.axis_size("sub")
    capacity = 2 * rows_dev // groups
    unit_rows = unit_of(embeddings, features)
    labels = cluster_ids[:, 0]
    member_table = (labels[:, None] == jnp.arange(groups, dtype=jnp.int32)[None, :]).astype(
        jnp.int32
    )
    running = jnp.cumsum(member_table, axis=0)
    within = jnp.sum(jnp.where(member_table > 0, running - 1, 0), axis=1)
    slot_index = labels * capacity + within
    outgoing = jnp.zeros((groups * capacity, features), jnp.bfloat16).at[slot_index].set(unit_rows)
    occupied = jnp.zeros((groups * capacity,), jnp.int32).at[slot_index].set(1)
    arrived, arrived_present = (
        lax.all_to_all(
            outgoing.reshape(groups, capacity, features),
            "grp",
            split_axis=0,
            concat_axis=0,
            tiled=True,
        ),
        lax.all_to_all(
            occupied.reshape(groups, capacity), "grp", split_axis=0, concat_axis=0, tiled=True
        ),
    )
    owned_rows = arrived.reshape(groups * capacity, features)
    present = arrived_present.reshape(groups * capacity)
    held = owned_rows.shape[0]
    positions = jnp.arange(held, dtype=jnp.int32)
    excluded = positions[:, None] == positions[None, :]
    highest = jnp.max(masked_maxima(owned_rows, owned_rows, present, excluded), axis=1)
    no_exclusion = jnp.zeros((held, held), dtype=bool)
    for offset in range(1, subgroup // 2 + 1):
        peer_rows, peer_present = from_behind((owned_rows, present), "sub", offset)
        scores = masked_maxima(owned_rows, peer_rows, peer_present, no_exclusion)
        highest = jnp.maximum(highest, jnp.max(scores, axis=1))
        if 2 * offset != subgroup:
            column_best = jnp.max(
                jnp.where(present[:, None] > 0, scores, jnp.float32(-1.0)), axis=0
            )
            returned_best = from_behind(column_best, "sub", -offset)
            highest = jnp.maximum(highest, returned_best)
    returned = lax.all_to_all(
        highest.reshape(groups, capacity), "grp", split_axis=0, concat_axis=0, tiled=True
    )
    return returned.reshape(groups * capacity)[slot_index]


LAG1 = (7, 4, 4, 4)
LAG2 = (1, 0, 4, 4, 2)
REST0 = 1
HOME = (5, 9)
LEAD = (3, 7)
FAR1 = (7, 9)
EARLY1 = (4, 6)
AHEAD = (6, 4)
SKIP = 1


def meet_kernel(
    groups, subgroup, chunks, pieces,
    emb_ref, ids_ref, out_ref,
    emb_in, level, foreign, relay, lane_ids, level_ids, ids_col, row_part, col_part,
    ret_out, ret_in, col_out, col_in,
    in_sem, ids_in, ids_send, ids_recv, lid_recv,
    lvl_send, lvl_recv, mate_recv, own_send, pass_send, relay_send,
    first_recv, second_recv, bulk_recv, relay_recv, ret_send, col_recv,
):
    rows, features = emb_ref.shape
    size = rows // chunks
    load = rows // pieces
    far0 = chunks // 4
    near0 = chunks - far0
    unit = chunks // 16
    skip = SKIP * unit
    pivot = groups // 2
    last = groups - 1
    rep = lax.axis_index("rep")
    depth = lax.axis_index("grp")
    z = depth * (1 - rep) + (last - depth) * rep
    s = lax.axis_index("sub")
    far1 = unit * (FAR1[0] * (1 - rep) + FAR1[1] * rep)
    near1 = chunks - far1
    their_far1 = unit * (FAR1[1] * (1 - rep) + FAR1[0] * rep)
    their_near1 = chunks - their_far1
    early1 = unit * (EARLY1[0] * (1 - rep) + EARLY1[1] * rep)
    their_early1 = unit * (EARLY1[1] * (1 - rep) + EARLY1[0] * rep)
    partner = s + 1 - 2 * lax.rem(s, 2)
    others = subgroup // 2
    across_y = {"rep": 1 - rep}

    def peer(k):
        return lax.rem(s + k, subgroup)

    def at(where):
        return {"grp": where * (1 - rep) + (last - where) * rep}

    def remote(src, dst, send, recv, where):
        return pltpu.make_async_remote_copy(
            src_ref=src, dst_ref=dst, send_sem=send, recv_sem=recv,
            device_id=where, device_id_type=MESH,
        )

    def slot(b):
        return pl.ds(pl.multiple_of(b * rows, rows), rows)

    def piece(b, p):
        return pl.ds(pl.multiple_of(b * rows + p * load, load), load)

    def own_chunk(k):
        return level.at[pl.ds(pl.multiple_of(s * rows + k * size, size), size), :]

    def part(k):
        return pl.ds(pl.multiple_of(k * size, size), size)

    def load_piece(p):
        where = pl.ds(pl.multiple_of(p * load, load), load)
        return pltpu.make_async_copy(emb_ref.at[where, :], emb_in.at[where, :], in_sem.at[p])

    turn = jnp.where(z == 0, pieces - 1, 0)

    def turned(p):
        return lax.rem(p + turn, pieces)

    load_piece(turned(0)).start()
    barrier = pltpu.get_barrier_semaphore()

    @pl.when(z > 0)
    def _():
        pl.semaphore_signal(barrier, 1, device_id=at(z - 1), device_id_type=MESH)

    @pl.when(z < last)
    def _():
        pl.semaphore_signal(barrier, 1, device_id=at(z + 1), device_id_type=MESH)

    @pl.when(z == last)
    def _():
        pl.semaphore_signal(barrier, 1, device_id=at(z - 1) | across_y, device_id_type=MESH)

    pl.semaphore_signal(barrier, 1, device_id=across_y, device_id_type=MESH)
    for k in range(1, subgroup):
        pl.semaphore_signal(barrier, 1, device_id={"sub": peer(k)}, device_id_type=MESH)

    for p in range(1, pieces):
        load_piece(turned(p)).start()
    ids_copy = pltpu.make_async_copy(ids_ref, level_ids.at[s], ids_in)
    ids_copy.start()

    col_part[...] = jnp.full(col_part.shape, -1.0, jnp.float32)
    row_part[...] = jnp.full(row_part.shape, -1.0, jnp.float32)

    def level_ids_copy(k):
        return remote(ids_ref, level_ids.at[s], ids_send, lid_recv, {"sub": peer(k)})

    def own_ids(where):
        return remote(ids_ref, lane_ids.at[z], ids_send, ids_recv.at[z], at(where))

    def ids_on(i, where):
        return remote(lane_ids.at[i], lane_ids.at[i], ids_send, ids_recv.at[i], at(where))

    def bytes_of(count, send, recv):
        block = level.at[pl.ds(0, count), :]
        return remote(block, block, send, recv, {"sub": peer(1)})

    back0, back1, block3 = range(3)
    far1_recv, far0a, far0b, rest0 = range(4)
    ahead = unit * (AHEAD[0] * (1 - rep) + AHEAD[1] * rep)
    lead1 = unit * (LEAD[0] * (1 - rep) + LEAD[1] * rep)

    def own_along(k, where, recv):
        return remote(own_chunk(k), foreign.at[z, part(k), :], own_send, recv, at(where))

    def own_across(i, k, j):
        return remote(own_chunk(k), relay.at[i, part(k), :], own_send, relay_recv.at[j], across_y)

    def passed_on(i, k, where, recv):
        block = foreign.at[i, part(k), :]
        return remote(block, block, pass_send, recv, at(where))

    def relayed(i, k, j):
        block = relay.at[i, part(k), :]
        return remote(block, block, relay_send, relay_recv.at[j], at(z - 1))

    def returned(i, k, where):
        return remote(
            relay.at[i, part(k), :], foreign.at[i, part(k), :], relay_send, bulk_recv.at[back0 + i], where
        )

    def level_piece(owner, p, recv, where):
        block = level.at[piece(owner, p), :]
        return remote(block, block, lvl_send, recv, {"sub": where})

    sends_right = z < pivot
    sends_left = z == last

    def start_own(k):
        @pl.when((z == 0) & (k < near0))
        def _():
            own_along(k, z + 1, first_recv.at[k]).start()

        @pl.when((z == 0) & (k >= near0))
        def _():
            own_across(0, k, early1 + k - near0).start()

        @pl.when((z == 1) & (k < lead1))
        def _():
            own_along(k, z + 1, second_recv.at[k]).start()

        @pl.when((z == 1) & (k >= near1))
        def _():
            own_across(1, k, k - near1 + jnp.where(k < near1 + early1, 0, far0)).start()

        @pl.when((z == last) & (k < ahead))
        def _():
            own_along(k, z - 1, bulk_recv.at[block3]).start()

    step = rows // 8
    per_piece = load // step
    per_load = load // size

    def normalize(h):
        where = pl.ds(pl.multiple_of(h * step, step), step)
        into = pl.ds(pl.multiple_of(s * rows + h * step, step), step)
        level[into, :] = unit_of(emb_in[where, :], features)

    def send_own(p):
        @pl.when(z != pivot)
        def _():
            lax.fori_loop(
                per_load * p, per_load * (p + 1), lambda k, c: (start_own(k), c)[1], 0
            )

        for k in range(1, others):
            level_piece(s, p, lvl_recv.at[k - 1, p], peer(2 * k)).start()
        level_piece(s, p, mate_recv.at[0], partner).start()

    load_piece(turn).wait()
    lax.fori_loop(
        turn * per_piece, (turn + 1) * per_piece, lambda h, c: (normalize(h), c)[1], 0
    )
    neighbours = subgroup + sum(c.astype(jnp.int32) for c in (z > 0, z < last, z == 1))
    pl.semaphore_wait(barrier, neighbours)

    @pl.when(sends_right)
    def _():
        own_ids(z + 1).start()

    @pl.when(sends_left)
    def _():
        own_ids(z - 1).start()

    send_own(turn)
    for k in range(1, subgroup):
        level_ids_copy(k).start()

    def norm_step(q, carry):
        p = turned(q)
        load_piece(p).wait()
        lax.fori_loop(p * per_piece, (p + 1) * per_piece, lambda h, c: (normalize(h), c)[1], 0)
        send_own(p)
        return carry

    lax.fori_loop(1, pieces, norm_step, 0)
    ids_copy.wait()

    def level_forward(q):
        p = turned(q)
        for k in range(1, others):
            arrived = level_piece(peer(subgroup - 2 * k), p, lvl_recv.at[k - 1, p], s)
            arrived.wait_recv()
            level_piece(peer(subgroup - 2 * k), p, mate_recv.at[1], partner).start()

    def relay_step(j):
        block = jnp.where((j < their_early1) | (j >= their_early1 + far0), 1, 0)
        chunk = j + jnp.where(
            j < their_early1, their_near1, jnp.where(j < their_early1 + far0, near0 - their_early1, their_near1 - far0)
        )
        hold = relayed(block, chunk, j)
        hold.wait_recv()

        @pl.when(z >= pivot)
        def _():
            hold.start()

        @pl.when(z == 1)
        def _():
            returned(block, chunk, across_y).start()
            returned(block, chunk, at(z - 1) | across_y).start()

    crossing = far0 + their_far1
    stride = chunks // pieces

    def ticks(count, native, lag_relay, lag_level):
        def tick(t, carry):
            native(t)
            j = t - lag_relay

            @pl.when((j >= 0) & (j < crossing))
            def _():
                relay_step(j)

            p = t - lag_level

            @pl.when((p >= 0) & (lax.rem(p, stride) == 0) & (p < pieces * stride))
            def _():
                level_forward(p // stride)

            return carry

        lax.fori_loop(0, count, tick, 0)

    def either_way(body):
        for way, far in enumerate(FAR1):
            @pl.when(rep == way)
            def _(far=far):
                body(far * unit)

    def wait_bulk(index, count, among=bulk_recv):
        bytes_of(count * size, relay_send, among.at[index]).wait_recv()

    def spread(i, ids):
        ids_col[i] = jnp.broadcast_to(ids, (LANES, rows)).T

    def wait_home():
        bytes_of(rows, lvl_send, mate_recv.at[0]).wait_recv()
        remote(
            level_ids.at[pl.ds(0, subgroup - 1)], level_ids.at[pl.ds(0, subgroup - 1)],
            ids_send, lid_recv, {"sub": peer(1)},
        ).wait_recv()
        spread(z, level_ids[s])

    def wait_away():
        bytes_of((others - 1) * rows, lvl_send, mate_recv.at[1]).wait_recv()

    def meet(i, low, high, chip, own=False):
        meet_rows(((i, low, high),), chip, own)

    def meet_rows(parts, chip, own=False):
        side = lax.rem(s // 2 + chip, others) * 2
        start = side * rows
        if own:
            block = level[slot(s), :]
        else:
            block = jnp.concatenate([foreign[i, low:high, :] for i, low, high in parts], axis=0)
        others_rows = level[pl.ds(pl.multiple_of(start, 2 * rows), 2 * rows), :]
        similar = lax.dot_general(
            block, others_rows, (((1,), (1,)), ((), ())), preferred_element_type=jnp.float32
        )
        top = 0
        for i, low, high in parts:
            count = high - low
            own_ids = ids_col[i, low:high, :]
            best = row_part[i, low:high, :]
            for col in range(0, 2 * rows, LANES):
                same = own_ids == level_ids[side + col // rows, :, col % rows : col % rows + LANES]
                if own:
                    across = lax.broadcasted_iota(jnp.int32, (rows, LANES), 1) + (col + start)
                    down = lax.broadcasted_iota(jnp.int32, (rows, LANES), 0) + s * rows
                    same = same & (across != down)
                kept = jnp.where(
                    same, similar[top : top + count, col : col + LANES], jnp.float32(-1.0)
                )
                best = jnp.maximum(best, kept)
                if not own:
                    columns = jnp.max(kept.reshape(count // SUBLANES, SUBLANES, LANES), axis=0)
                    where = pl.ds(pl.multiple_of(start + col, LANES), LANES)
                    col_part[:, where] = jnp.maximum(col_part[:, where], columns)
            row_part[i, low:high, :] = best
            top += count

    def meet_all(i, low, high, own=False):
        for chip in range(others):
            meet(i, low, high, chip, own)

    def flat(i):
        return jnp.max(row_part[i].T, axis=0, keepdims=True)

    def ret_copy(i, owner, where):
        return remote(ret_out.at[i], ret_in.at[owner], ret_send, second_recv.at[groups + owner], at(where))

    def columns_of(b):
        where = pl.ds(pl.multiple_of(b * rows, rows), rows)
        return jnp.max(col_part[:, where], axis=0, keepdims=True)

    def send_columns(b):
        col_out[b] = columns_of(b)
        remote(col_out.at[b], col_in.at[s], ret_send, col_recv, {"sub": b}).start()

    def give(i):
        ret_out[i] = flat(i)
        ret_copy(i, z, i).start()

    def finish(parts, blocks):
        for chip in range(1, others):
            meet_rows(parts, chip)
            for b in range(2):
                send_columns(lax.rem(s // 2 + chip, others) * 2 + b)
        meet_rows(parts, 0)
        for i in blocks:
            give(i)
        send_columns(partner)

    half = rows // 2

    @pl.when(z == last)
    def _():
        lax.fori_loop(
            their_early1, their_early1 + far0, lambda j, c: (relay_step(j), c)[1], 0
        )
        lax.fori_loop(
            ahead, chunks, lambda k, c: (own_along(k, z - 1, bulk_recv.at[block3]).start(), c)[1], 0
        )

    @pl.when((z == 0) | (z == last))
    def _():
        def early(p, carry):
            level_forward(p)

            @pl.when((z == 0) & (p == REST0))
            def _():
                lax.fori_loop(
                    near0, chunks,
                    lambda k, c: (own_along(k, z + 1, second_recv.at[rest0]).start(), c)[1], 0,
                )

            @pl.when(p == pieces // 2)
            def _():
                wait_home()
                meet(z, 0, rows, 0, True)

            return carry

        lax.fori_loop(0, pieces, early, 0)
        wait_away()
        for chip in range(1, others):
            meet(z, 0, rows, chip, True)

    @pl.when(z == 1)
    def _():
        ids_on(0, z).wait_recv()
        ids_on(0, z + 1).start()

        def native(t):
            @pl.when(t < near0)
            def _():
                passed_on(0, t, z, first_recv.at[t]).wait_recv()

                @pl.when((rep == 1) & (t >= near0 - skip))
                def _():
                    passed_on(0, t, z + 2, second_recv.at[far0b]).start()

                passed_on(0, t, z + 1, first_recv.at[t]).start()

            @pl.when(t == near0 - 1)
            def _():
                def late(k, carry):
                    @pl.when((rep == 0) & (k >= near1 - skip))
                    def _():
                        own_along(k, z + 2, second_recv.at[far1_recv]).start()

                    own_along(k, z + 1, second_recv.at[k]).start()
                    return carry

                lax.fori_loop(lead1, near1, late, 0)

        ticks(
            max(LAG1[0] * unit + far0 + max(FAR1) * unit, (LAG1[2] + 12) * unit + 1), native,
            unit * (LAG1[0] * (1 - rep) + LAG1[1] * rep),
            unit * (LAG1[2] * (1 - rep) + LAG1[3] * rep),
        )
        wait_home()
        wait_away()
        spread(0, lane_ids[0])
        wait_bulk(rest0, far0, second_recv)
        finish(((0, 0, rows),), (0,))
        meet_all(z, 0, rows, True)

    @pl.when(z == pivot)
    def _():
        ids_on(1, z).wait_recv()
        ids_on(1, z + 1).start()
        lead = LAG2[4] * unit

        def meet_first():
            spread(0, lane_ids[0])
            wait_bulk(back0, far0)
            meet_all(0, 0, rows)
            give(0)

        def own_away():
            for chip in range(1, others):
                meet(z, 0, rows, chip, True)

        steps = near1 + near0

        def native(t):
            k = t - lead * rep

            m = k - lead1
            own = k - jnp.where(k < lead1, 0, near0)

            @pl.when((k >= 0) & (k < lead1) | (k >= lead1 + near0) & (k < steps))
            def _():
                passed_on(1, own, z, second_recv.at[own]).wait_recv()

                @pl.when((rep == 1) | (own < near1 - skip))
                def _():
                    passed_on(1, own, z + 1, second_recv.at[far1_recv]).start()

            @pl.when(m == 0)
            def _():
                ids_on(0, z).wait_recv()
                ids_on(0, z + 1).start()

            @pl.when((m >= 0) & (m < near0))
            def _():
                passed_on(0, m, z, first_recv.at[m]).wait_recv()

            @pl.when((m >= 0) & (m < chunks // 2))
            def _():
                passed_on(0, m, z + 1, second_recv.at[far0a]).start()

            @pl.when((m >= chunks // 2) & (m < near0 - skip * rep))
            def _():
                passed_on(0, m, z + 1, second_recv.at[far0b]).start()

            @pl.when(k == steps - unit * (HOME[0] * (1 - rep) + HOME[1] * rep))
            def _():
                wait_home()
                meet(z, 0, rows, 0, True)

            @pl.when((k == steps - 2 * unit) & (rep == 0))
            def _():
                wait_away()
                meet_first()

            @pl.when((k == steps - 2 * unit) & (rep == 1))
            def _():
                wait_away()
                own_away()

        ticks(
            steps + lead, native,
            unit * (LAG2[0] * (1 - rep) + LAG2[1] * rep),
            unit * (LAG2[2] * (1 - rep) + LAG2[3] * rep),
        )
        def await_last():
            ids_on(last, z).wait_recv()
            spread(last, lane_ids[last])
            wait_bulk(block3, chunks)

        @pl.when(rep == 1)
        def _():
            await_last()
            meet_all(last, 0, rows)
            give(last)
            meet_first()

        spread(1, lane_ids[1])
        either_way(lambda far: wait_bulk(back1, far))

        @pl.when(rep == 0)
        def _():
            meet_all(1, 0, rows)
            give(1)
            await_last()
            finish(((last, 0, rows),), (last,))
            own_away()

        @pl.when(rep == 1)
        def _():
            finish(((1, 0, rows),), (1,))

    @pl.when(z == last)
    def _():
        ids_on(0, z).wait_recv()
        spread(0, lane_ids[0])
        ids_on(1, z).wait_recv()
        spread(1, lane_ids[1])

        def first_half():
            wait_bulk(far0a, chunks // 2, second_recv)
            meet_all(0, 0, half)

        def await_second_half():
            wait_bulk(far0b, near0 - chunks // 2, second_recv)
            wait_bulk(back0, far0)

        @pl.when(rep == 0)
        def _():
            first_half()
            await_second_half()
            meet_all(0, half, rows)
            give(0)
            wait_bulk(back1, FAR1[0] * unit)
            wait_bulk(far1_recv, chunks - FAR1[0] * unit, second_recv)
            meet_all(1, 0, rows)
            give(1)
            for k in range(1, subgroup):
                send_columns(peer(k))

        @pl.when(rep == 1)
        def _():
            near = chunks - FAR1[1] * unit
            wait_bulk(far1_recv, near, second_recv)
            meet_all(1, 0, near * size)
            first_half()
            await_second_half()
            wait_bulk(back1, FAR1[1] * unit)
            finish(((0, half, rows), (1, near * size, rows)), (1, 0))

    out_ref[...] = flat(z).reshape(rows)

    bytes_of(2 * (others - 1) * rows + rows, lvl_send, col_recv).wait_send()

    def sent_ids(count):
        block = lane_ids.at[pl.ds(0, count)]
        remote(block, block, ids_send, col_recv, {"sub": peer(1)}).wait_send()

    @pl.when((z == 0) | (z == last))
    def _():
        sent_ids(subgroup)

    @pl.when((z > 0) & (z < last))
    def _():
        sent_ids(subgroup + 1)

    @pl.when(z == 0)
    def _():
        bytes_of((chunks + far0) * size, own_send, col_recv).wait_send()

    @pl.when(z == 1)
    def _():
        for way in (0, 1):
            @pl.when(rep == way)
            def _(way=way):
                bytes_of((chunks + skip * (1 - way)) * size, own_send, col_recv).wait_send()
                bytes_of((near0 + skip * way) * size, pass_send, col_recv).wait_send()

    @pl.when(z == last)
    def _():
        bytes_of(rows, own_send, col_recv).wait_send()
        bytes_of(far0 * size, relay_send, col_recv).wait_send()

    @pl.when(z == 1)
    def _():
        either_way(
            lambda far: bytes_of(
                2 * (far0 + sum(FAR1) * unit - far) * size, relay_send, col_recv
            ).wait_send()
        )

    @pl.when(z == pivot)
    def _():
        either_way(
            lambda far: bytes_of((chunks - far - skip + near0) * size, pass_send, col_recv).wait_send()
        )
        either_way(
            lambda far: bytes_of(
                (far0 + sum(FAR1) * unit - far) * size, relay_send, col_recv
            ).wait_send()
        )

    @pl.when(z > 0)
    def _():
        block = col_in.at[pl.ds(0, subgroup - 1)]
        remote(block, block, ret_send, col_recv, {"sub": peer(1)}).wait_recv()
        heard = columns_of(s)
        for k in range(1, subgroup):
            heard = jnp.maximum(heard, col_in[peer(k)])
        out_ref[...] = jnp.maximum(out_ref[...], heard.reshape(rows))

    for j in range(1, groups):
        @pl.when((z < j) & (z < pivot) | (z > j) & (z > pivot) & (j >= pivot))
        def _(j=j):
            ret_copy(0, j, z).wait_recv()
            out_ref[...] = jnp.maximum(out_ref[...], ret_in[j].reshape(rows))

    def sent_maxima(count):
        block = col_in.at[pl.ds(0, count)]
        remote(block, block, ret_send, col_recv, {"sub": peer(1)}).wait_send()

    for here, count in ((1, 1), (pivot, 3), (last, 2)):
        @pl.when(z == here)
        def _(count=count):
            sent_maxima(subgroup - 1 + count)


def by_meeting(embeddings, cluster_ids, chunks, pieces):
    rows, features = embeddings.shape
    groups = lax.axis_size("grp")
    subgroup = lax.axis_size("sub")
    dma = pltpu.SemaphoreType.DMA
    return pl.pallas_call(
        functools.partial(meet_kernel, groups, subgroup, chunks, pieces),
        out_shape=pltpu.VMEM((rows,), jnp.float32),
        in_specs=[pl.BlockSpec(memory_space=pl.ANY)] * 2,
        out_specs=pl.BlockSpec(memory_space=pltpu.VMEM),
        scratch_shapes=[
            pltpu.VMEM((rows, features), jnp.bfloat16),
            pltpu.VMEM((subgroup * rows, features), jnp.bfloat16),
            pltpu.VMEM((groups, rows, features), jnp.bfloat16),
            pltpu.VMEM((groups // 2, rows, features), jnp.bfloat16),
            pltpu.VMEM((2 * subgroup, 1, rows), jnp.int32),
            pltpu.VMEM((subgroup, 1, rows), jnp.int32),
            pltpu.VMEM((groups, rows, LANES), jnp.int32),
            pltpu.VMEM((groups, rows, LANES), jnp.float32),
            pltpu.VMEM((SUBLANES, subgroup * rows), jnp.float32),
            pltpu.VMEM((groups, 1, rows), jnp.float32),
            pltpu.VMEM((groups, 1, rows), jnp.float32),
            pltpu.VMEM((subgroup, 1, rows), jnp.float32),
            pltpu.VMEM((2 * subgroup, 1, rows), jnp.float32),
            dma((pieces,)), dma, dma, dma((groups,)), dma,
            dma, dma((max(subgroup // 2 - 1, 1), pieces)), dma((2,)), dma, dma, dma,
            dma((3 * chunks // 4,)), dma((max(chunks - min(FAR1) * chunks // 16, 2 * groups),)), dma((3,)),
            dma((chunks // 4 + max(FAR1) * chunks // 16,)),
            dma, dma,
        ],
        compiler_params=pltpu.CompilerParams(collective_id=0, has_side_effects=True),
    )(embeddings, cluster_ids.reshape(1, rows))


def local(embeddings, cluster_ids):
    rows, features = embeddings.shape
    groups = lax.axis_size("grp")
    subgroup = lax.axis_size("sub")
    held = (groups + subgroup) * rows * features * embeddings.dtype.itemsize
    paired = lax.axis_size("rep") == 2 and subgroup % 2 == 0 and groups == 4
    if held <= VMEM_BUDGET and paired and rows % (LANES * 2) == 0:
        return by_meeting(embeddings, cluster_ids, rows // 16, 4)
    return by_owner(embeddings, cluster_ids)


def solution(mesh):
    return jax.shard_map(
        local,
        mesh=mesh,
        in_specs=(P(("rep", "grp", "sub"), None), P(("rep", "grp", "sub"), None)),
        out_specs=P(("rep", "grp", "sub")),
        check_vma=False,
    )
```

```python
import functools
import math

import jax
import jax.numpy as jnp
from jax import lax
from jax.experimental import pallas as pl
from jax.experimental.pallas import tpu as pltpu
from jax.sharding import PartitionSpec as P

LANES = 128
SUBLANES = 8
VMEM_BUDGET = 24 << 20
MESH = pl.DeviceIdType.MESH


def from_behind(value, axis, by):
    peers = lax.axis_size(axis)
    return lax.ppermute(value, axis, [(i, (i + by) % peers) for i in range(peers)])


def masked_maxima(left_rows, right_rows, right_present, excluded):
    similar = jnp.dot(left_rows, right_rows.T, preferred_element_type=jnp.float32)
    allowed = (right_present[None, :] > 0) & jnp.logical_not(excluded)
    return jnp.where(allowed, similar, jnp.float32(-1.0))


def unit_of(rows, features):
    floats = rows.astype(jnp.float32)
    return (
        floats
        * lax.rsqrt(jnp.mean(floats * floats, axis=1, keepdims=True) + 1e-06)
        / math.sqrt(features)
    ).astype(jnp.bfloat16)


def by_owner(embeddings, cluster_ids):
    rows_dev, features = embeddings.shape
    groups = lax.axis_size("grp")
    subgroup = lax.axis_size("sub")
    capacity = 2 * rows_dev // groups
    unit_rows = unit_of(embeddings, features)
    labels = cluster_ids[:, 0]
    member_table = (labels[:, None] == jnp.arange(groups, dtype=jnp.int32)[None, :]).astype(
        jnp.int32
    )
    running = jnp.cumsum(member_table, axis=0)
    within = jnp.sum(jnp.where(member_table > 0, running - 1, 0), axis=1)
    slot_index = labels * capacity + within
    outgoing = jnp.zeros((groups * capacity, features), jnp.bfloat16).at[slot_index].set(unit_rows)
    occupied = jnp.zeros((groups * capacity,), jnp.int32).at[slot_index].set(1)
    arrived, arrived_present = (
        lax.all_to_all(
            outgoing.reshape(groups, capacity, features),
            "grp",
            split_axis=0,
            concat_axis=0,
            tiled=True,
        ),
        lax.all_to_all(
            occupied.reshape(groups, capacity), "grp", split_axis=0, concat_axis=0, tiled=True
        ),
    )
    owned_rows = arrived.reshape(groups * capacity, features)
    present = arrived_present.reshape(groups * capacity)
    held = owned_rows.shape[0]
    positions = jnp.arange(held, dtype=jnp.int32)
    excluded = positions[:, None] == positions[None, :]
    highest = jnp.max(masked_maxima(owned_rows, owned_rows, present, excluded), axis=1)
    no_exclusion = jnp.zeros((held, held), dtype=bool)
    for offset in range(1, subgroup // 2 + 1):
        peer_rows, peer_present = from_behind((owned_rows, present), "sub", offset)
        scores = masked_maxima(owned_rows, peer_rows, peer_present, no_exclusion)
        highest = jnp.maximum(highest, jnp.max(scores, axis=1))
        if 2 * offset != subgroup:
            column_best = jnp.max(
                jnp.where(present[:, None] > 0, scores, jnp.float32(-1.0)), axis=0
            )
            returned_best = from_behind(column_best, "sub", -offset)
            highest = jnp.maximum(highest, returned_best)
    returned = lax.all_to_all(
        highest.reshape(groups, capacity), "grp", split_axis=0, concat_axis=0, tiled=True
    )
    return returned.reshape(groups * capacity)[slot_index]


LAG1 = (7, 4, 4, 4)
LAG2 = (1, 0, 4, 4, 1)
REST0 = 1
HOME = (5, 9)
LEAD = (3, 7)
FAR1 = (7, 9)
EARLY1 = (4, 6)
AHEAD = (6, 4)
SKIP = 1


def meet_kernel(
    groups, subgroup, chunks, pieces,
    emb_ref, ids_ref, out_ref,
    emb_in, level, foreign, relay, lane_ids, level_ids, ids_col, row_part, col_part,
    ret_out, ret_in, col_out, col_in,
    in_sem, ids_in, ids_send, ids_recv, lid_recv,
    lvl_send, lvl_recv, mate_recv, own_send, pass_send, relay_send,
    first_recv, second_recv, bulk_recv, relay_recv, ret_send, col_recv,
):
    rows, features = emb_ref.shape
    size = rows // chunks
    load = rows // pieces
    far0 = chunks // 4
    near0 = chunks - far0
    unit = chunks // 16
    skip = SKIP * unit
    pivot = groups // 2
    last = groups - 1
    rep = lax.axis_index("rep")
    depth = lax.axis_index("grp")
    z = depth * (1 - rep) + (last - depth) * rep
    s = lax.axis_index("sub")
    far1 = unit * (FAR1[0] * (1 - rep) + FAR1[1] * rep)
    near1 = chunks - far1
    their_far1 = unit * (FAR1[1] * (1 - rep) + FAR1[0] * rep)
    their_near1 = chunks - their_far1
    early1 = unit * (EARLY1[0] * (1 - rep) + EARLY1[1] * rep)
    their_early1 = unit * (EARLY1[1] * (1 - rep) + EARLY1[0] * rep)
    partner = s + 1 - 2 * lax.rem(s, 2)
    others = subgroup // 2
    across_y = {"rep": 1 - rep}

    def peer(k):
        return lax.rem(s + k, subgroup)

    def at(where):
        return {"grp": where * (1 - rep) + (last - where) * rep}

    def remote(src, dst, send, recv, where):
        return pltpu.make_async_remote_copy(
            src_ref=src, dst_ref=dst, send_sem=send, recv_sem=recv,
            device_id=where, device_id_type=MESH,
        )

    def slot(b):
        return pl.ds(pl.multiple_of(b * rows, rows), rows)

    def piece(b, p):
        return pl.ds(pl.multiple_of(b * rows + p * load, load), load)

    def own_chunk(k):
        return level.at[pl.ds(pl.multiple_of(s * rows + k * size, size), size), :]

    def part(k):
        return pl.ds(pl.multiple_of(k * size, size), size)

    def load_piece(p):
        where = pl.ds(pl.multiple_of(p * load, load), load)
        return pltpu.make_async_copy(emb_ref.at[where, :], emb_in.at[where, :], in_sem.at[p])

    turn = jnp.where(z == 0, pieces - 1, 0)

    def turned(p):
        return lax.rem(p + turn, pieces)

    load_piece(turned(0)).start()
    barrier = pltpu.get_barrier_semaphore()

    @pl.when(z > 0)
    def _():
        pl.semaphore_signal(barrier, 1, device_id=at(z - 1), device_id_type=MESH)

    @pl.when(z < last)
    def _():
        pl.semaphore_signal(barrier, 1, device_id=at(z + 1), device_id_type=MESH)

    @pl.when(z == last)
    def _():
        pl.semaphore_signal(barrier, 1, device_id=at(z - 1) | across_y, device_id_type=MESH)

    pl.semaphore_signal(barrier, 1, device_id=across_y, device_id_type=MESH)
    for k in range(1, subgroup):
        pl.semaphore_signal(barrier, 1, device_id={"sub": peer(k)}, device_id_type=MESH)

    for p in range(1, pieces):
        load_piece(turned(p)).start()
    ids_copy = pltpu.make_async_copy(ids_ref, level_ids.at[s], ids_in)
    ids_copy.start()

    col_part[...] = jnp.full(col_part.shape, -1.0, jnp.float32)
    row_part[...] = jnp.full(row_part.shape, -1.0, jnp.float32)

    def level_ids_copy(k):
        return remote(ids_ref, level_ids.at[s], ids_send, lid_recv, {"sub": peer(k)})

    def own_ids(where):
        return remote(ids_ref, lane_ids.at[z], ids_send, ids_recv.at[z], at(where))

    def ids_on(i, where):
        return remote(lane_ids.at[i], lane_ids.at[i], ids_send, ids_recv.at[i], at(where))

    def bytes_of(count, send, recv):
        block = level.at[pl.ds(0, count), :]
        return remote(block, block, send, recv, {"sub": peer(1)})

    back0, back1, block3 = range(3)
    far1_recv, far0a, far0b, rest0 = range(4)
    ahead = unit * (AHEAD[0] * (1 - rep) + AHEAD[1] * rep)
    lead1 = unit * (LEAD[0] * (1 - rep) + LEAD[1] * rep)

    def own_along(k, where, recv):
        return remote(own_chunk(k), foreign.at[z, part(k), :], own_send, recv, at(where))

    def own_across(i, k, j):
        return remote(own_chunk(k), relay.at[i, part(k), :], own_send, relay_recv.at[j], across_y)

    def passed_on(i, k, where, recv):
        block = foreign.at[i, part(k), :]
        return remote(block, block, pass_send, recv, at(where))

    def relayed(i, k, j):
        block = relay.at[i, part(k), :]
        return remote(block, block, relay_send, relay_recv.at[j], at(z - 1))

    def returned(i, k, where):
        return remote(
            relay.at[i, part(k), :], foreign.at[i, part(k), :], relay_send, bulk_recv.at[back0 + i], where
        )

    def level_piece(owner, p, recv, where):
        block = level.at[piece(owner, p), :]
        return remote(block, block, lvl_send, recv, {"sub": where})

    sends_right = z < pivot
    sends_left = z == last

    def start_own(k):
        @pl.when((z == 0) & (k < near0))
        def _():
            own_along(k, z + 1, first_recv.at[k]).start()

        @pl.when((z == 0) & (k >= near0))
        def _():
            own_across(0, k, early1 + k - near0).start()

        @pl.when((z == 1) & (k < lead1))
        def _():
            own_along(k, z + 1, second_recv.at[k]).start()

        @pl.when((z == 1) & (k >= near1))
        def _():
            own_across(1, k, k - near1 + jnp.where(k < near1 + early1, 0, far0)).start()

        @pl.when((z == last) & (k < ahead))
        def _():
            own_along(k, z - 1, bulk_recv.at[block3]).start()

    step = rows // 8
    per_piece = load // step
    per_load = load // size

    def normalize(h):
        where = pl.ds(pl.multiple_of(h * step, step), step)
        into = pl.ds(pl.multiple_of(s * rows + h * step, step), step)
        level[into, :] = unit_of(emb_in[where, :], features)

    def send_own(p):
        @pl.when(z != pivot)
        def _():
            lax.fori_loop(
                per_load * p, per_load * (p + 1), lambda k, c: (start_own(k), c)[1], 0
            )

        for k in range(1, others):
            level_piece(s, p, lvl_recv.at[k - 1, p], peer(2 * k)).start()
        level_piece(s, p, mate_recv.at[0], partner).start()

    load_piece(turn).wait()
    lax.fori_loop(
        turn * per_piece, (turn + 1) * per_piece, lambda h, c: (normalize(h), c)[1], 0
    )
    neighbours = subgroup + sum(c.astype(jnp.int32) for c in (z > 0, z < last, z == 1))
    pl.semaphore_wait(barrier, neighbours)

    @pl.when(sends_right)
    def _():
        own_ids(z + 1).start()

    @pl.when(sends_left)
    def _():
        own_ids(z - 1).start()

    send_own(turn)
    for k in range(1, subgroup):
        level_ids_copy(k).start()

    def norm_step(q, carry):
        p = turned(q)
        load_piece(p).wait()
        lax.fori_loop(p * per_piece, (p + 1) * per_piece, lambda h, c: (normalize(h), c)[1], 0)
        send_own(p)
        return carry

    lax.fori_loop(1, pieces, norm_step, 0)
    ids_copy.wait()

    def level_forward(q):
        p = turned(q)
        for k in range(1, others):
            arrived = level_piece(peer(subgroup - 2 * k), p, lvl_recv.at[k - 1, p], s)
            arrived.wait_recv()
            level_piece(peer(subgroup - 2 * k), p, mate_recv.at[1], partner).start()

    def relay_step(j):
        block = jnp.where((j < their_early1) | (j >= their_early1 + far0), 1, 0)
        chunk = j + jnp.where(
            j < their_early1, their_near1, jnp.where(j < their_early1 + far0, near0 - their_early1, their_near1 - far0)
        )
        hold = relayed(block, chunk, j)
        hold.wait_recv()

        @pl.when(z >= pivot)
        def _():
            hold.start()

        @pl.when(z == 1)
        def _():
            returned(block, chunk, across_y).start()
            returned(block, chunk, at(z - 1) | across_y).start()

    crossing = far0 + their_far1
    stride = chunks // pieces

    def ticks(count, native, lag_relay, lag_level):
        def tick(t, carry):
            native(t)
            j = t - lag_relay

            @pl.when((j >= 0) & (j < crossing))
            def _():
                relay_step(j)

            p = t - lag_level

            @pl.when((p >= 0) & (lax.rem(p, stride) == 0) & (p < pieces * stride))
            def _():
                level_forward(p // stride)

            return carry

        lax.fori_loop(0, count, tick, 0)

    def either_way(body):
        for way, far in enumerate(FAR1):
            @pl.when(rep == way)
            def _(far=far):
                body(far * unit)

    def wait_bulk(index, count, among=bulk_recv):
        bytes_of(count * size, relay_send, among.at[index]).wait_recv()

    def spread(i, ids):
        ids_col[i] = jnp.broadcast_to(ids, (LANES, rows)).T

    def wait_home():
        bytes_of(rows, lvl_send, mate_recv.at[0]).wait_recv()
        remote(
            level_ids.at[pl.ds(0, subgroup - 1)], level_ids.at[pl.ds(0, subgroup - 1)],
            ids_send, lid_recv, {"sub": peer(1)},
        ).wait_recv()
        spread(z, level_ids[s])

    def wait_away():
        bytes_of((others - 1) * rows, lvl_send, mate_recv.at[1]).wait_recv()

    def meet(i, low, high, chip, own=False):
        meet_rows(((i, low, high),), chip, own)

    def meet_rows(parts, chip, own=False):
        side = lax.rem(s // 2 + chip, others) * 2
        start = side * rows
        if own:
            block = level[slot(s), :]
        else:
            block = jnp.concatenate([foreign[i, low:high, :] for i, low, high in parts], axis=0)
        others_rows = level[pl.ds(pl.multiple_of(start, 2 * rows), 2 * rows), :]
        similar = lax.dot_general(
            block, others_rows, (((1,), (1,)), ((), ())), preferred_element_type=jnp.float32
        )
        top = 0
        for i, low, high in parts:
            count = high - low
            own_ids = ids_col[i, low:high, :]
            best = row_part[i, low:high, :]
            for col in range(0, 2 * rows, LANES):
                same = own_ids == level_ids[side + col // rows, :, col % rows : col % rows + LANES]
                if own:
                    across = lax.broadcasted_iota(jnp.int32, (rows, LANES), 1) + (col + start)
                    down = lax.broadcasted_iota(jnp.int32, (rows, LANES), 0) + s * rows
                    same = same & (across != down)
                kept = jnp.where(
                    same, similar[top : top + count, col : col + LANES], jnp.float32(-1.0)
                )
                best = jnp.maximum(best, kept)
                if not own:
                    columns = jnp.max(kept.reshape(count // SUBLANES, SUBLANES, LANES), axis=0)
                    where = pl.ds(pl.multiple_of(start + col, LANES), LANES)
                    col_part[:, where] = jnp.maximum(col_part[:, where], columns)
            row_part[i, low:high, :] = best
            top += count

    def meet_all(i, low, high, own=False):
        for chip in range(others):
            meet(i, low, high, chip, own)

    def flat(i):
        return jnp.max(row_part[i].T, axis=0, keepdims=True)

    def ret_copy(i, owner, where):
        return remote(ret_out.at[i], ret_in.at[owner], ret_send, second_recv.at[groups + owner], at(where))

    def columns_of(b):
        where = pl.ds(pl.multiple_of(b * rows, rows), rows)
        return jnp.max(col_part[:, where], axis=0, keepdims=True)

    def send_columns(b):
        col_out[b] = columns_of(b)
        remote(col_out.at[b], col_in.at[s], ret_send, col_recv, {"sub": b}).start()

    def give(i):
        ret_out[i] = flat(i)
        ret_copy(i, z, i).start()

    def finish(parts, blocks):
        for chip in range(1, others):
            meet_rows(parts, chip)
            for b in range(2):
                send_columns(lax.rem(s // 2 + chip, others) * 2 + b)
        meet_rows(parts, 0)
        for i in blocks:
            give(i)
        send_columns(partner)

    half = rows // 2

    @pl.when(z == last)
    def _():
        lax.fori_loop(
            their_early1, their_early1 + far0, lambda j, c: (relay_step(j), c)[1], 0
        )
        lax.fori_loop(
            ahead, chunks, lambda k, c: (own_along(k, z - 1, bulk_recv.at[block3]).start(), c)[1], 0
        )

    @pl.when((z == 0) | (z == last))
    def _():
        def early(p, carry):
            level_forward(p)

            @pl.when((z == 0) & (p == REST0))
            def _():
                lax.fori_loop(
                    near0, chunks,
                    lambda k, c: (own_along(k, z + 1, second_recv.at[rest0]).start(), c)[1], 0,
                )

            @pl.when(p == pieces // 2)
            def _():
                wait_home()
                meet(z, 0, rows, 0, True)

            return carry

        lax.fori_loop(0, pieces, early, 0)
        wait_away()
        for chip in range(1, others):
            meet(z, 0, rows, chip, True)

    @pl.when(z == 1)
    def _():
        ids_on(0, z).wait_recv()
        ids_on(0, z + 1).start()

        def native(t):
            @pl.when(t < near0)
            def _():
                passed_on(0, t, z, first_recv.at[t]).wait_recv()

                @pl.when((rep == 1) & (t >= near0 - skip))
                def _():
                    passed_on(0, t, z + 2, second_recv.at[far0b]).start()

                passed_on(0, t, z + 1, first_recv.at[t]).start()

            @pl.when(t == near0 - 1)
            def _():
                def late(k, carry):
                    @pl.when((rep == 0) & (k >= near1 - skip))
                    def _():
                        own_along(k, z + 2, second_recv.at[far1_recv]).start()

                    own_along(k, z + 1, second_recv.at[k]).start()
                    return carry

                lax.fori_loop(lead1, near1, late, 0)

        ticks(
            max(LAG1[0] * unit + far0 + max(FAR1) * unit, (LAG1[2] + 12) * unit + 1), native,
            unit * (LAG1[0] * (1 - rep) + LAG1[1] * rep),
            unit * (LAG1[2] * (1 - rep) + LAG1[3] * rep),
        )
        wait_home()
        wait_away()
        spread(0, lane_ids[0])
        wait_bulk(rest0, far0, second_recv)
        finish(((0, 0, rows),), (0,))
        meet_all(z, 0, rows, True)

    @pl.when(z == pivot)
    def _():
        ids_on(1, z).wait_recv()
        ids_on(1, z + 1).start()
        lead = LAG2[4] * unit

        def meet_first():
            spread(0, lane_ids[0])
            wait_bulk(back0, far0)
            meet_all(0, 0, rows)
            give(0)

        def own_away():
            for chip in range(1, others):
                meet(z, 0, rows, chip, True)

        steps = near1 + near0

        def native(t):
            k = t - lead * rep

            m = k - lead1
            own = k - jnp.where(k < lead1, 0, near0)

            @pl.when((k >= 0) & (k < lead1) | (k >= lead1 + near0) & (k < steps))
            def _():
                passed_on(1, own, z, second_recv.at[own]).wait_recv()

                @pl.when((rep == 1) | (own < near1 - skip))
                def _():
                    passed_on(1, own, z + 1, second_recv.at[far1_recv]).start()

            @pl.when(m == 0)
            def _():
                ids_on(0, z).wait_recv()
                ids_on(0, z + 1).start()

            @pl.when((m >= 0) & (m < near0))
            def _():
                passed_on(0, m, z, first_recv.at[m]).wait_recv()

            @pl.when((m >= 0) & (m < chunks // 2))
            def _():
                passed_on(0, m, z + 1, second_recv.at[far0a]).start()

            @pl.when((m >= chunks // 2) & (m < near0 - skip * rep))
            def _():
                passed_on(0, m, z + 1, second_recv.at[far0b]).start()

            @pl.when(k == steps - unit * (HOME[0] * (1 - rep) + HOME[1] * rep))
            def _():
                wait_home()
                meet(z, 0, rows, 0, True)

            @pl.when((k == steps - 2 * unit) & (rep == 0))
            def _():
                wait_away()
                meet_first()

            @pl.when((k == steps - 2 * unit) & (rep == 1))
            def _():
                wait_away()
                own_away()

        ticks(
            steps + lead, native,
            unit * (LAG2[0] * (1 - rep) + LAG2[1] * rep),
            unit * (LAG2[2] * (1 - rep) + LAG2[3] * rep),
        )
        def await_last():
            ids_on(last, z).wait_recv()
            spread(last, lane_ids[last])
            wait_bulk(block3, chunks)

        @pl.when(rep == 1)
        def _():
            await_last()
            meet_all(last, 0, rows)
            give(last)
            meet_first()

        spread(1, lane_ids[1])
        either_way(lambda far: wait_bulk(back1, far))

        @pl.when(rep == 0)
        def _():
            meet_all(1, 0, rows)
            give(1)
            await_last()
            finish(((last, 0, rows),), (last,))
            own_away()

        @pl.when(rep == 1)
        def _():
            finish(((1, 0, rows),), (1,))

    @pl.when(z == last)
    def _():
        ids_on(0, z).wait_recv()
        spread(0, lane_ids[0])
        ids_on(1, z).wait_recv()
        spread(1, lane_ids[1])

        def first_half():
            wait_bulk(far0a, chunks // 2, second_recv)
            meet_all(0, 0, half)

        def await_second_half():
            wait_bulk(far0b, near0 - chunks // 2, second_recv)
            wait_bulk(back0, far0)

        @pl.when(rep == 0)
        def _():
            first_half()
            await_second_half()
            meet_all(0, half, rows)
            give(0)
            wait_bulk(back1, FAR1[0] * unit)
            wait_bulk(far1_recv, chunks - FAR1[0] * unit, second_recv)
            meet_all(1, 0, rows)
            give(1)
            for k in range(1, subgroup):
                send_columns(peer(k))

        @pl.when(rep == 1)
        def _():
            near = chunks - FAR1[1] * unit
            wait_bulk(far1_recv, near, second_recv)
            meet_all(1, 0, near * size)
            first_half()
            await_second_half()
            wait_bulk(back1, FAR1[1] * unit)
            finish(((0, half, rows), (1, near * size, rows)), (1, 0))

    out_ref[...] = flat(z).reshape(rows)

    bytes_of(2 * (others - 1) * rows + rows, lvl_send, col_recv).wait_send()

    def sent_ids(count):
        block = lane_ids.at[pl.ds(0, count)]
        remote(block, block, ids_send, col_recv, {"sub": peer(1)}).wait_send()

    @pl.when((z == 0) | (z == last))
    def _():
        sent_ids(subgroup)

    @pl.when((z > 0) & (z < last))
    def _():
        sent_ids(subgroup + 1)

    @pl.when(z == 0)
    def _():
        bytes_of((chunks + far0) * size, own_send, col_recv).wait_send()

    @pl.when(z == 1)
    def _():
        for way in (0, 1):
            @pl.when(rep == way)
            def _(way=way):
                bytes_of((chunks + skip * (1 - way)) * size, own_send, col_recv).wait_send()
                bytes_of((near0 + skip * way) * size, pass_send, col_recv).wait_send()

    @pl.when(z == last)
    def _():
        bytes_of(rows, own_send, col_recv).wait_send()
        bytes_of(far0 * size, relay_send, col_recv).wait_send()

    @pl.when(z == 1)
    def _():
        either_way(
            lambda far: bytes_of(
                2 * (far0 + sum(FAR1) * unit - far) * size, relay_send, col_recv
            ).wait_send()
        )

    @pl.when(z == pivot)
    def _():
        either_way(
            lambda far: bytes_of((chunks - far - skip + near0) * size, pass_send, col_recv).wait_send()
        )
        either_way(
            lambda far: bytes_of(
                (far0 + sum(FAR1) * unit - far) * size, relay_send, col_recv
            ).wait_send()
        )

    @pl.when(z > 0)
    def _():
        block = col_in.at[pl.ds(0, subgroup - 1)]
        remote(block, block, ret_send, col_recv, {"sub": peer(1)}).wait_recv()
        heard = columns_of(s)
        for k in range(1, subgroup):
            heard = jnp.maximum(heard, col_in[peer(k)])
        out_ref[...] = jnp.maximum(out_ref[...], heard.reshape(rows))

    for j in range(1, groups):
        @pl.when((z < j) & (z < pivot) | (z > j) & (z > pivot) & (j >= pivot))
        def _(j=j):
            ret_copy(0, j, z).wait_recv()
            out_ref[...] = jnp.maximum(out_ref[...], ret_in[j].reshape(rows))

    def sent_maxima(count):
        block = col_in.at[pl.ds(0, count)]
        remote(block, block, ret_send, col_recv, {"sub": peer(1)}).wait_send()

    for here, count in ((1, 1), (pivot, 3), (last, 2)):
        @pl.when(z == here)
        def _(count=count):
            sent_maxima(subgroup - 1 + count)


def by_meeting(embeddings, cluster_ids, chunks, pieces):
    rows, features = embeddings.shape
    groups = lax.axis_size("grp")
    subgroup = lax.axis_size("sub")
    dma = pltpu.SemaphoreType.DMA
    return pl.pallas_call(
        functools.partial(meet_kernel, groups, subgroup, chunks, pieces),
        out_shape=pltpu.VMEM((rows,), jnp.float32),
        in_specs=[pl.BlockSpec(memory_space=pl.ANY)] * 2,
        out_specs=pl.BlockSpec(memory_space=pltpu.VMEM),
        scratch_shapes=[
            pltpu.VMEM((rows, features), jnp.bfloat16),
            pltpu.VMEM((subgroup * rows, features), jnp.bfloat16),
            pltpu.VMEM((groups, rows, features), jnp.bfloat16),
            pltpu.VMEM((groups // 2, rows, features), jnp.bfloat16),
            pltpu.VMEM((2 * subgroup, 1, rows), jnp.int32),
            pltpu.VMEM((subgroup, 1, rows), jnp.int32),
            pltpu.VMEM((groups, rows, LANES), jnp.int32),
            pltpu.VMEM((groups, rows, LANES), jnp.float32),
            pltpu.VMEM((SUBLANES, subgroup * rows), jnp.float32),
            pltpu.VMEM((groups, 1, rows), jnp.float32),
            pltpu.VMEM((groups, 1, rows), jnp.float32),
            pltpu.VMEM((subgroup, 1, rows), jnp.float32),
            pltpu.VMEM((2 * subgroup, 1, rows), jnp.float32),
            dma((pieces,)), dma, dma, dma((groups,)), dma,
            dma, dma((max(subgroup // 2 - 1, 1), pieces)), dma((2,)), dma, dma, dma,
            dma((3 * chunks // 4,)), dma((max(chunks - min(FAR1) * chunks // 16, 2 * groups),)), dma((3,)),
            dma((chunks // 4 + max(FAR1) * chunks // 16,)),
            dma, dma,
        ],
        compiler_params=pltpu.CompilerParams(collective_id=0, has_side_effects=True),
    )(embeddings, cluster_ids.reshape(1, rows))


def local(embeddings, cluster_ids):
    rows, features = embeddings.shape
    groups = lax.axis_size("grp")
    subgroup = lax.axis_size("sub")
    held = (groups + subgroup) * rows * features * embeddings.dtype.itemsize
    paired = lax.axis_size("rep") == 2 and subgroup % 2 == 0 and groups == 4
    if held <= VMEM_BUDGET and paired and rows % (LANES * 2) == 0:
        return by_meeting(embeddings, cluster_ids, rows // 16, 4)
    return by_owner(embeddings, cluster_ids)


def solution(mesh):
    return jax.shard_map(
        local,
        mesh=mesh,
        in_specs=(P(("rep", "grp", "sub"), None), P(("rep", "grp", "sub"), None)),
        out_specs=P(("rep", "grp", "sub")),
        check_vma=False,
    )
```

```python
import functools
import math

import jax
import jax.numpy as jnp
from jax import lax
from jax.experimental import pallas as pl
from jax.experimental.pallas import tpu as pltpu
from jax.sharding import PartitionSpec as P

LANES = 128
SUBLANES = 8
VMEM_BUDGET = 24 << 20
MESH = pl.DeviceIdType.MESH


def from_behind(value, axis, by):
    peers = lax.axis_size(axis)
    return lax.ppermute(value, axis, [(i, (i + by) % peers) for i in range(peers)])


def masked_maxima(left_rows, right_rows, right_present, excluded):
    similar = jnp.dot(left_rows, right_rows.T, preferred_element_type=jnp.float32)
    allowed = (right_present[None, :] > 0) & jnp.logical_not(excluded)
    return jnp.where(allowed, similar, jnp.float32(-1.0))


def unit_of(rows, features):
    floats = rows.astype(jnp.float32)
    return (
        floats
        * lax.rsqrt(jnp.mean(floats * floats, axis=1, keepdims=True) + 1e-06)
        / math.sqrt(features)
    ).astype(jnp.bfloat16)


def by_owner(embeddings, cluster_ids):
    rows_dev, features = embeddings.shape
    groups = lax.axis_size("grp")
    subgroup = lax.axis_size("sub")
    capacity = 2 * rows_dev // groups
    unit_rows = unit_of(embeddings, features)
    labels = cluster_ids[:, 0]
    member_table = (labels[:, None] == jnp.arange(groups, dtype=jnp.int32)[None, :]).astype(
        jnp.int32
    )
    running = jnp.cumsum(member_table, axis=0)
    within = jnp.sum(jnp.where(member_table > 0, running - 1, 0), axis=1)
    slot_index = labels * capacity + within
    outgoing = jnp.zeros((groups * capacity, features), jnp.bfloat16).at[slot_index].set(unit_rows)
    occupied = jnp.zeros((groups * capacity,), jnp.int32).at[slot_index].set(1)
    arrived, arrived_present = (
        lax.all_to_all(
            outgoing.reshape(groups, capacity, features),
            "grp",
            split_axis=0,
            concat_axis=0,
            tiled=True,
        ),
        lax.all_to_all(
            occupied.reshape(groups, capacity), "grp", split_axis=0, concat_axis=0, tiled=True
        ),
    )
    owned_rows = arrived.reshape(groups * capacity, features)
    present = arrived_present.reshape(groups * capacity)
    held = owned_rows.shape[0]
    positions = jnp.arange(held, dtype=jnp.int32)
    excluded = positions[:, None] == positions[None, :]
    highest = jnp.max(masked_maxima(owned_rows, owned_rows, present, excluded), axis=1)
    no_exclusion = jnp.zeros((held, held), dtype=bool)
    for offset in range(1, subgroup // 2 + 1):
        peer_rows, peer_present = from_behind((owned_rows, present), "sub", offset)
        scores = masked_maxima(owned_rows, peer_rows, peer_present, no_exclusion)
        highest = jnp.maximum(highest, jnp.max(scores, axis=1))
        if 2 * offset != subgroup:
            column_best = jnp.max(
                jnp.where(present[:, None] > 0, scores, jnp.float32(-1.0)), axis=0
            )
            returned_best = from_behind(column_best, "sub", -offset)
            highest = jnp.maximum(highest, returned_best)
    returned = lax.all_to_all(
        highest.reshape(groups, capacity), "grp", split_axis=0, concat_axis=0, tiled=True
    )
    return returned.reshape(groups * capacity)[slot_index]


LAG1 = (7, 4, 4, 4)
LAG2 = (1, 0, 4, 4, 1)
REST0 = 1
HOME = (5, 9)
LEAD = (3, 7)
FAR1 = (7, 9)
EARLY1 = (4, 6)
AHEAD = (5, 3)
SKIP = 1


def meet_kernel(
    groups, subgroup, chunks, pieces,
    emb_ref, ids_ref, out_ref,
    emb_in, level, foreign, relay, lane_ids, level_ids, ids_col, row_part, col_part,
    ret_out, ret_in, col_out, col_in,
    in_sem, ids_in, ids_send, ids_recv, lid_recv,
    lvl_send, lvl_recv, mate_recv, own_send, pass_send, relay_send,
    first_recv, second_recv, bulk_recv, relay_recv, ret_send, col_recv,
):
    rows, features = emb_ref.shape
    size = rows // chunks
    load = rows // pieces
    far0 = chunks // 4
    near0 = chunks - far0
    unit = chunks // 16
    skip = SKIP * unit
    pivot = groups // 2
    last = groups - 1
    rep = lax.axis_index("rep")
    depth = lax.axis_index("grp")
    z = depth * (1 - rep) + (last - depth) * rep
    s = lax.axis_index("sub")
    far1 = unit * (FAR1[0] * (1 - rep) + FAR1[1] * rep)
    near1 = chunks - far1
    their_far1 = unit * (FAR1[1] * (1 - rep) + FAR1[0] * rep)
    their_near1 = chunks - their_far1
    early1 = unit * (EARLY1[0] * (1 - rep) + EARLY1[1] * rep)
    their_early1 = unit * (EARLY1[1] * (1 - rep) + EARLY1[0] * rep)
    partner = s + 1 - 2 * lax.rem(s, 2)
    others = subgroup // 2
    across_y = {"rep": 1 - rep}

    def peer(k):
        return lax.rem(s + k, subgroup)

    def at(where):
        return {"grp": where * (1 - rep) + (last - where) * rep}

    def remote(src, dst, send, recv, where):
        return pltpu.make_async_remote_copy(
            src_ref=src, dst_ref=dst, send_sem=send, recv_sem=recv,
            device_id=where, device_id_type=MESH,
        )

    def slot(b):
        return pl.ds(pl.multiple_of(b * rows, rows), rows)

    def piece(b, p):
        return pl.ds(pl.multiple_of(b * rows + p * load, load), load)

    def own_chunk(k):
        return level.at[pl.ds(pl.multiple_of(s * rows + k * size, size), size), :]

    def part(k):
        return pl.ds(pl.multiple_of(k * size, size), size)

    def load_piece(p):
        where = pl.ds(pl.multiple_of(p * load, load), load)
        return pltpu.make_async_copy(emb_ref.at[where, :], emb_in.at[where, :], in_sem.at[p])

    turn = jnp.where(z == 0, pieces - 1, 0)

    def turned(p):
        return lax.rem(p + turn, pieces)

    load_piece(turned(0)).start()
    barrier = pltpu.get_barrier_semaphore()

    @pl.when(z > 0)
    def _():
        pl.semaphore_signal(barrier, 1, device_id=at(z - 1), device_id_type=MESH)

    @pl.when(z < last)
    def _():
        pl.semaphore_signal(barrier, 1, device_id=at(z + 1), device_id_type=MESH)

    @pl.when(z == last)
    def _():
        pl.semaphore_signal(barrier, 1, device_id=at(z - 1) | across_y, device_id_type=MESH)

    pl.semaphore_signal(barrier, 1, device_id=across_y, device_id_type=MESH)
    for k in range(1, subgroup):
        pl.semaphore_signal(barrier, 1, device_id={"sub": peer(k)}, device_id_type=MESH)

    for p in range(1, pieces):
        load_piece(turned(p)).start()
    ids_copy = pltpu.make_async_copy(ids_ref, level_ids.at[s], ids_in)
    ids_copy.start()

    col_part[...] = jnp.full(col_part.shape, -1.0, jnp.float32)
    row_part[...] = jnp.full(row_part.shape, -1.0, jnp.float32)

    def level_ids_copy(k):
        return remote(ids_ref, level_ids.at[s], ids_send, lid_recv, {"sub": peer(k)})

    def own_ids(where):
        return remote(ids_ref, lane_ids.at[z], ids_send, ids_recv.at[z], at(where))

    def ids_on(i, where):
        return remote(lane_ids.at[i], lane_ids.at[i], ids_send, ids_recv.at[i], at(where))

    def bytes_of(count, send, recv):
        block = level.at[pl.ds(0, count), :]
        return remote(block, block, send, recv, {"sub": peer(1)})

    back0, back1, block3 = range(3)
    far1_recv, far0a, far0b, rest0 = range(4)
    ahead = unit * (AHEAD[0] * (1 - rep) + AHEAD[1] * rep)
    lead1 = unit * (LEAD[0] * (1 - rep) + LEAD[1] * rep)

    def own_along(k, where, recv):
        return remote(own_chunk(k), foreign.at[z, part(k), :], own_send, recv, at(where))

    def own_across(i, k, j):
        return remote(own_chunk(k), relay.at[i, part(k), :], own_send, relay_recv.at[j], across_y)

    def passed_on(i, k, where, recv):
        block = foreign.at[i, part(k), :]
        return remote(block, block, pass_send, recv, at(where))

    def relayed(i, k, j):
        block = relay.at[i, part(k), :]
        return remote(block, block, relay_send, relay_recv.at[j], at(z - 1))

    def returned(i, k, where):
        return remote(
            relay.at[i, part(k), :], foreign.at[i, part(k), :], relay_send, bulk_recv.at[back0 + i], where
        )

    def level_piece(owner, p, recv, where):
        block = level.at[piece(owner, p), :]
        return remote(block, block, lvl_send, recv, {"sub": where})

    sends_right = z < pivot
    sends_left = z == last

    def start_own(k):
        @pl.when((z == 0) & (k < near0))
        def _():
            own_along(k, z + 1, first_recv.at[k]).start()

        @pl.when((z == 0) & (k >= near0))
        def _():
            own_across(0, k, early1 + k - near0).start()

        @pl.when((z == 1) & (k < lead1))
        def _():
            own_along(k, z + 1, second_recv.at[k]).start()

        @pl.when((z == 1) & (k >= near1))
        def _():
            own_across(1, k, k - near1 + jnp.where(k < near1 + early1, 0, far0)).start()

        @pl.when((z == last) & (k < ahead))
        def _():
            own_along(k, z - 1, bulk_recv.at[block3]).start()

    step = rows // 8
    per_piece = load // step
    per_load = load // size

    def normalize(h):
        where = pl.ds(pl.multiple_of(h * step, step), step)
        into = pl.ds(pl.multiple_of(s * rows + h * step, step), step)
        level[into, :] = unit_of(emb_in[where, :], features)

    def send_own(p):
        @pl.when(z != pivot)
        def _():
            lax.fori_loop(
                per_load * p, per_load * (p + 1), lambda k, c: (start_own(k), c)[1], 0
            )

        for k in range(1, others):
            level_piece(s, p, lvl_recv.at[k - 1, p], peer(2 * k)).start()
        level_piece(s, p, mate_recv.at[0], partner).start()

    load_piece(turn).wait()
    lax.fori_loop(
        turn * per_piece, (turn + 1) * per_piece, lambda h, c: (normalize(h), c)[1], 0
    )
    neighbours = subgroup + sum(c.astype(jnp.int32) for c in (z > 0, z < last, z == 1))
    pl.semaphore_wait(barrier, neighbours)

    @pl.when(sends_right)
    def _():
        own_ids(z + 1).start()

    @pl.when(sends_left)
    def _():
        own_ids(z - 1).start()

    send_own(turn)
    for k in range(1, subgroup):
        level_ids_copy(k).start()

    def norm_step(q, carry):
        p = turned(q)
        load_piece(p).wait()
        lax.fori_loop(p * per_piece, (p + 1) * per_piece, lambda h, c: (normalize(h), c)[1], 0)
        send_own(p)
        return carry

    lax.fori_loop(1, pieces, norm_step, 0)
    ids_copy.wait()

    def level_forward(q):
        p = turned(q)
        for k in range(1, others):
            arrived = level_piece(peer(subgroup - 2 * k), p, lvl_recv.at[k - 1, p], s)
            arrived.wait_recv()
            level_piece(peer(subgroup - 2 * k), p, mate_recv.at[1], partner).start()

    def relay_step(j):
        block = jnp.where((j < their_early1) | (j >= their_early1 + far0), 1, 0)
        chunk = j + jnp.where(
            j < their_early1, their_near1, jnp.where(j < their_early1 + far0, near0 - their_early1, their_near1 - far0)
        )
        hold = relayed(block, chunk, j)
        hold.wait_recv()

        @pl.when(z >= pivot)
        def _():
            hold.start()

        @pl.when(z == 1)
        def _():
            returned(block, chunk, across_y).start()
            returned(block, chunk, at(z - 1) | across_y).start()

    crossing = far0 + their_far1
    stride = chunks // pieces

    def ticks(count, native, lag_relay, lag_level):
        def tick(t, carry):
            native(t)
            j = t - lag_relay

            @pl.when((j >= 0) & (j < crossing))
            def _():
                relay_step(j)

            p = t - lag_level

            @pl.when((p >= 0) & (lax.rem(p, stride) == 0) & (p < pieces * stride))
            def _():
                level_forward(p // stride)

            return carry

        lax.fori_loop(0, count, tick, 0)

    def either_way(body):
        for way, far in enumerate(FAR1):
            @pl.when(rep == way)
            def _(far=far):
                body(far * unit)

    def wait_bulk(index, count, among=bulk_recv):
        bytes_of(count * size, relay_send, among.at[index]).wait_recv()

    def spread(i, ids):
        ids_col[i] = jnp.broadcast_to(ids, (LANES, rows)).T

    def wait_home():
        bytes_of(rows, lvl_send, mate_recv.at[0]).wait_recv()
        remote(
            level_ids.at[pl.ds(0, subgroup - 1)], level_ids.at[pl.ds(0, subgroup - 1)],
            ids_send, lid_recv, {"sub": peer(1)},
        ).wait_recv()
        spread(z, level_ids[s])

    def wait_away():
        bytes_of((others - 1) * rows, lvl_send, mate_recv.at[1]).wait_recv()

    def meet(i, low, high, chip, own=False):
        meet_rows(((i, low, high),), chip, own)

    def meet_rows(parts, chip, own=False):
        side = lax.rem(s // 2 + chip, others) * 2
        start = side * rows
        if own:
            block = level[slot(s), :]
        else:
            block = jnp.concatenate([foreign[i, low:high, :] for i, low, high in parts], axis=0)
        others_rows = level[pl.ds(pl.multiple_of(start, 2 * rows), 2 * rows), :]
        similar = lax.dot_general(
            block, others_rows, (((1,), (1,)), ((), ())), preferred_element_type=jnp.float32
        )
        top = 0
        for i, low, high in parts:
            count = high - low
            own_ids = ids_col[i, low:high, :]
            best = row_part[i, low:high, :]
            for col in range(0, 2 * rows, LANES):
                same = own_ids == level_ids[side + col // rows, :, col % rows : col % rows + LANES]
                if own:
                    across = lax.broadcasted_iota(jnp.int32, (rows, LANES), 1) + (col + start)
                    down = lax.broadcasted_iota(jnp.int32, (rows, LANES), 0) + s * rows
                    same = same & (across != down)
                kept = jnp.where(
                    same, similar[top : top + count, col : col + LANES], jnp.float32(-1.0)
                )
                best = jnp.maximum(best, kept)
                if not own:
                    columns = jnp.max(kept.reshape(count // SUBLANES, SUBLANES, LANES), axis=0)
                    where = pl.ds(pl.multiple_of(start + col, LANES), LANES)
                    col_part[:, where] = jnp.maximum(col_part[:, where], columns)
            row_part[i, low:high, :] = best
            top += count

    def meet_all(i, low, high, own=False):
        for chip in range(others):
            meet(i, low, high, chip, own)

    def flat(i):
        return jnp.max(row_part[i].T, axis=0, keepdims=True)

    def ret_copy(i, owner, where):
        return remote(ret_out.at[i], ret_in.at[owner], ret_send, second_recv.at[groups + owner], at(where))

    def columns_of(b):
        where = pl.ds(pl.multiple_of(b * rows, rows), rows)
        return jnp.max(col_part[:, where], axis=0, keepdims=True)

    def send_columns(b):
        col_out[b] = columns_of(b)
        remote(col_out.at[b], col_in.at[s], ret_send, col_recv, {"sub": b}).start()

    def give(i):
        ret_out[i] = flat(i)
        ret_copy(i, z, i).start()

    def finish(parts, blocks):
        for chip in range(1, others):
            meet_rows(parts, chip)
            for b in range(2):
                send_columns(lax.rem(s // 2 + chip, others) * 2 + b)
        meet_rows(parts, 0)
        for i in blocks:
            give(i)
        send_columns(partner)

    half = rows // 2

    @pl.when(z == last)
    def _():
        lax.fori_loop(
            their_early1, their_early1 + far0, lambda j, c: (relay_step(j), c)[1], 0
        )
        lax.fori_loop(
            ahead, chunks, lambda k, c: (own_along(k, z - 1, bulk_recv.at[block3]).start(), c)[1], 0
        )

    @pl.when((z == 0) | (z == last))
    def _():
        def early(p, carry):
            level_forward(p)

            @pl.when((z == 0) & (p == REST0))
            def _():
                lax.fori_loop(
                    near0, chunks,
                    lambda k, c: (own_along(k, z + 1, second_recv.at[rest0]).start(), c)[1], 0,
                )

            @pl.when(p == pieces // 2)
            def _():
                wait_home()
                meet(z, 0, rows, 0, True)

            return carry

        lax.fori_loop(0, pieces, early, 0)
        wait_away()
        for chip in range(1, others):
            meet(z, 0, rows, chip, True)

    @pl.when(z == 1)
    def _():
        ids_on(0, z).wait_recv()
        ids_on(0, z + 1).start()

        def native(t):
            @pl.when(t < near0)
            def _():
                passed_on(0, t, z, first_recv.at[t]).wait_recv()

                @pl.when((rep == 1) & (t >= near0 - skip))
                def _():
                    passed_on(0, t, z + 2, second_recv.at[far0b]).start()

                passed_on(0, t, z + 1, first_recv.at[t]).start()

            @pl.when(t == near0 - 1)
            def _():
                def late(k, carry):
                    @pl.when((rep == 0) & (k >= near1 - skip))
                    def _():
                        own_along(k, z + 2, second_recv.at[far1_recv]).start()

                    own_along(k, z + 1, second_recv.at[k]).start()
                    return carry

                lax.fori_loop(lead1, near1, late, 0)

        ticks(
            max(LAG1[0] * unit + far0 + max(FAR1) * unit, (LAG1[2] + 12) * unit + 1), native,
            unit * (LAG1[0] * (1 - rep) + LAG1[1] * rep),
            unit * (LAG1[2] * (1 - rep) + LAG1[3] * rep),
        )
        wait_home()
        wait_away()
        spread(0, lane_ids[0])
        wait_bulk(rest0, far0, second_recv)
        finish(((0, 0, rows),), (0,))
        meet_all(z, 0, rows, True)

    @pl.when(z == pivot)
    def _():
        ids_on(1, z).wait_recv()
        ids_on(1, z + 1).start()
        lead = LAG2[4] * unit

        def meet_first():
            spread(0, lane_ids[0])
            wait_bulk(back0, far0)
            meet_all(0, 0, rows)
            give(0)

        def own_away():
            for chip in range(1, others):
                meet(z, 0, rows, chip, True)

        steps = near1 + near0

        def native(t):
            k = t - lead * rep

            m = k - lead1
            own = k - jnp.where(k < lead1, 0, near0)

            @pl.when((k >= 0) & (k < lead1) | (k >= lead1 + near0) & (k < steps))
            def _():
                passed_on(1, own, z, second_recv.at[own]).wait_recv()

                @pl.when((rep == 1) | (own < near1 - skip))
                def _():
                    passed_on(1, own, z + 1, second_recv.at[far1_recv]).start()

            @pl.when(m == 0)
            def _():
                ids_on(0, z).wait_recv()
                ids_on(0, z + 1).start()

            @pl.when((m >= 0) & (m < near0))
            def _():
                passed_on(0, m, z, first_recv.at[m]).wait_recv()

            @pl.when((m >= 0) & (m < chunks // 2))
            def _():
                passed_on(0, m, z + 1, second_recv.at[far0a]).start()

            @pl.when((m >= chunks // 2) & (m < near0 - skip * rep))
            def _():
                passed_on(0, m, z + 1, second_recv.at[far0b]).start()

            @pl.when(k == steps - unit * (HOME[0] * (1 - rep) + HOME[1] * rep))
            def _():
                wait_home()
                meet(z, 0, rows, 0, True)

            @pl.when((k == steps - 2 * unit) & (rep == 0))
            def _():
                wait_away()
                meet_first()

            @pl.when((k == steps - 2 * unit) & (rep == 1))
            def _():
                wait_away()
                own_away()

        ticks(
            steps + lead, native,
            unit * (LAG2[0] * (1 - rep) + LAG2[1] * rep),
            unit * (LAG2[2] * (1 - rep) + LAG2[3] * rep),
        )
        def await_last():
            ids_on(last, z).wait_recv()
            spread(last, lane_ids[last])
            wait_bulk(block3, chunks)

        @pl.when(rep == 1)
        def _():
            await_last()
            meet_all(last, 0, rows)
            give(last)
            meet_first()

        spread(1, lane_ids[1])
        either_way(lambda far: wait_bulk(back1, far))

        @pl.when(rep == 0)
        def _():
            meet_all(1, 0, rows)
            give(1)
            await_last()
            finish(((last, 0, rows),), (last,))
            own_away()

        @pl.when(rep == 1)
        def _():
            finish(((1, 0, rows),), (1,))

    @pl.when(z == last)
    def _():
        ids_on(0, z).wait_recv()
        spread(0, lane_ids[0])
        ids_on(1, z).wait_recv()
        spread(1, lane_ids[1])

        def first_half():
            wait_bulk(far0a, chunks // 2, second_recv)
            meet_all(0, 0, half)

        def await_second_half():
            wait_bulk(far0b, near0 - chunks // 2, second_recv)
            wait_bulk(back0, far0)

        @pl.when(rep == 0)
        def _():
            first_half()
            await_second_half()
            meet_all(0, half, rows)
            give(0)
            wait_bulk(back1, FAR1[0] * unit)
            wait_bulk(far1_recv, chunks - FAR1[0] * unit, second_recv)
            meet_all(1, 0, rows)
            give(1)
            for k in range(1, subgroup):
                send_columns(peer(k))

        @pl.when(rep == 1)
        def _():
            near = chunks - FAR1[1] * unit
            wait_bulk(far1_recv, near, second_recv)
            meet_all(1, 0, near * size)
            first_half()
            await_second_half()
            wait_bulk(back1, FAR1[1] * unit)
            finish(((0, half, rows), (1, near * size, rows)), (1, 0))

    out_ref[...] = flat(z).reshape(rows)

    bytes_of(2 * (others - 1) * rows + rows, lvl_send, col_recv).wait_send()

    def sent_ids(count):
        block = lane_ids.at[pl.ds(0, count)]
        remote(block, block, ids_send, col_recv, {"sub": peer(1)}).wait_send()

    @pl.when((z == 0) | (z == last))
    def _():
        sent_ids(subgroup)

    @pl.when((z > 0) & (z < last))
    def _():
        sent_ids(subgroup + 1)

    @pl.when(z == 0)
    def _():
        bytes_of((chunks + far0) * size, own_send, col_recv).wait_send()

    @pl.when(z == 1)
    def _():
        for way in (0, 1):
            @pl.when(rep == way)
            def _(way=way):
                bytes_of((chunks + skip * (1 - way)) * size, own_send, col_recv).wait_send()
                bytes_of((near0 + skip * way) * size, pass_send, col_recv).wait_send()

    @pl.when(z == last)
    def _():
        bytes_of(rows, own_send, col_recv).wait_send()
        bytes_of(far0 * size, relay_send, col_recv).wait_send()

    @pl.when(z == 1)
    def _():
        either_way(
            lambda far: bytes_of(
                2 * (far0 + sum(FAR1) * unit - far) * size, relay_send, col_recv
            ).wait_send()
        )

    @pl.when(z == pivot)
    def _():
        either_way(
            lambda far: bytes_of((chunks - far - skip + near0) * size, pass_send, col_recv).wait_send()
        )
        either_way(
            lambda far: bytes_of(
                (far0 + sum(FAR1) * unit - far) * size, relay_send, col_recv
            ).wait_send()
        )

    @pl.when(z > 0)
    def _():
        block = col_in.at[pl.ds(0, subgroup - 1)]
        remote(block, block, ret_send, col_recv, {"sub": peer(1)}).wait_recv()
        heard = columns_of(s)
        for k in range(1, subgroup):
            heard = jnp.maximum(heard, col_in[peer(k)])
        out_ref[...] = jnp.maximum(out_ref[...], heard.reshape(rows))

    for j in range(1, groups):
        @pl.when((z < j) & (z < pivot) | (z > j) & (z > pivot) & (j >= pivot))
        def _(j=j):
            ret_copy(0, j, z).wait_recv()
            out_ref[...] = jnp.maximum(out_ref[...], ret_in[j].reshape(rows))

    def sent_maxima(count):
        block = col_in.at[pl.ds(0, count)]
        remote(block, block, ret_send, col_recv, {"sub": peer(1)}).wait_send()

    for here, count in ((1, 1), (pivot, 3), (last, 2)):
        @pl.when(z == here)
        def _(count=count):
            sent_maxima(subgroup - 1 + count)


def by_meeting(embeddings, cluster_ids, chunks, pieces):
    rows, features = embeddings.shape
    groups = lax.axis_size("grp")
    subgroup = lax.axis_size("sub")
    dma = pltpu.SemaphoreType.DMA
    return pl.pallas_call(
        functools.partial(meet_kernel, groups, subgroup, chunks, pieces),
        out_shape=pltpu.VMEM((rows,), jnp.float32),
        in_specs=[pl.BlockSpec(memory_space=pl.ANY)] * 2,
        out_specs=pl.BlockSpec(memory_space=pltpu.VMEM),
        scratch_shapes=[
            pltpu.VMEM((rows, features), jnp.bfloat16),
            pltpu.VMEM((subgroup * rows, features), jnp.bfloat16),
            pltpu.VMEM((groups, rows, features), jnp.bfloat16),
            pltpu.VMEM((groups // 2, rows, features), jnp.bfloat16),
            pltpu.VMEM((2 * subgroup, 1, rows), jnp.int32),
            pltpu.VMEM((subgroup, 1, rows), jnp.int32),
            pltpu.VMEM((groups, rows, LANES), jnp.int32),
            pltpu.VMEM((groups, rows, LANES), jnp.float32),
            pltpu.VMEM((SUBLANES, subgroup * rows), jnp.float32),
            pltpu.VMEM((groups, 1, rows), jnp.float32),
            pltpu.VMEM((groups, 1, rows), jnp.float32),
            pltpu.VMEM((subgroup, 1, rows), jnp.float32),
            pltpu.VMEM((2 * subgroup, 1, rows), jnp.float32),
            dma((pieces,)), dma, dma, dma((groups,)), dma,
            dma, dma((max(subgroup // 2 - 1, 1), pieces)), dma((2,)), dma, dma, dma,
            dma((3 * chunks // 4,)), dma((max(chunks - min(FAR1) * chunks // 16, 2 * groups),)), dma((3,)),
            dma((chunks // 4 + max(FAR1) * chunks // 16,)),
            dma, dma,
        ],
        compiler_params=pltpu.CompilerParams(collective_id=0, has_side_effects=True),
    )(embeddings, cluster_ids.reshape(1, rows))


def local(embeddings, cluster_ids):
    rows, features = embeddings.shape
    groups = lax.axis_size("grp")
    subgroup = lax.axis_size("sub")
    held = (groups + subgroup) * rows * features * embeddings.dtype.itemsize
    paired = lax.axis_size("rep") == 2 and subgroup % 2 == 0 and groups == 4
    if held <= VMEM_BUDGET and paired and rows % (LANES * 2) == 0:
        return by_meeting(embeddings, cluster_ids, rows // 16, 4)
    return by_owner(embeddings, cluster_ids)


def solution(mesh):
    return jax.shard_map(
        local,
        mesh=mesh,
        in_specs=(P(("rep", "grp", "sub"), None), P(("rep", "grp", "sub"), None)),
        out_specs=P(("rep", "grp", "sub")),
        check_vma=False,
    )
```
